32 devices in a mesh: dp: 2 (over x), ctx: 4 (over y, core), tp: 4 (over z).
Axes of the slice: x: 2, y: 2, z: 4, core: 2. Of those that a mesh axis runs over, the one named last changes fastest.
Arguments:
- tokens: bfloat16 [2, 4096, 768], P('dp', 'ctx'), may hold values from -6 to 6
- time_steps: int32 [2], P('dp'), may hold values from 0 to 999
- lengths: int32 [2], P('dp'), may hold values from 2048 to 4096, as said below
- time_table: bfloat16 [1000, 768], P(None, 'dp'), may hold values from -3 to 3
- norm_gains: bfloat16 [2, 768], P(None, 'dp'), may hold values from 0.5 to 1.5
- norm_biases: bfloat16 [2, 768], P(None, 'dp'), may hold values from -1 to 1
- w_qkv: bfloat16 [3, 768, 768], P(None, 'dp', 'tp'), may hold values from -0.3125 to 0.3125
- b_qv: bfloat16 [2, 768], P(None, 'tp'), may hold values from -0.099609375 to 0.099609375
- w_out: bfloat16 [768, 768], P('tp', 'dp'), may hold values from -0.3125 to 0.3125
- out_biases: bfloat16 [2, 768], P(None, 'dp'), may hold values from -1.25 to 1.25
- w_up: bfloat16 [768, 3072], P('dp', 'tp'), may hold values from -0.21875 to 0.21875
- b_up: bfloat16 [3072], P('tp'), may hold values from -1 to 1
- w_down: bfloat16 [3072, 768], P('tp', 'dp'), may hold values from -0.109375 to 0.109375
- cotangent: bfloat16 [2, 4096, 768], P('dp', 'ctx'), may hold values from -6 to 6
Outputs:
- layer_out: bfloat16 [2, 4096, 768], P('dp', 'ctx')
- grad_tokens: float32 [2, 4096, 768], P('dp', 'ctx')
- grad_time_table: float32 [1000, 768], P(None, 'dp')
- grad_norm_gains: float32 [2, 768], P(None, 'dp')
- grad_norm_biases: float32 [2, 768], P(None, 'dp')
- grad_w_qkv: float32 [3, 768, 768], P(None, 'dp', 'tp')
- grad_b_qv: float32 [2, 768], P(None, 'tp')
- grad_w_out: float32 [768, 768], P('tp', 'dp')
- grad_out_biases: float32 [2, 768], P(None, 'dp')
- grad_w_up: float32 [768, 3072], P('dp', 'tp')
- grad_b_up: float32 [3072], P('tp')
- grad_w_down: float32 [3072, 768], P('tp', 'dp')
The draws below stay inside these ranges and needn't reach their ends.
Inputs may be any that keep to these rules, and one draw needn't show every extreme that they name: `lengths`: every sequence has 2048 to 4096 real tokens at its start, the rest padding; some sequence has exactly 4096.
All inputs are finite; a program needn't handle non-finite values.
Results may differ from the reference program's by a relative error of at most 0.019.
Values may be sent and summed in bfloat16 or wider, within the bound.
No kernel may reach another device: no remote copies, remote signals or barrier semaphores. Data moves between devices by JAX's collectives and lax.ppermute only.
A program may use at most 128 MiB of HBM per device.

```python
import jax
import jax.numpy as jnp
from jax import lax

D = 768
HEADS = 12
HEAD = 64
FF = 3072
TSTEPS = 1000
LEN = 4096
SEQS = 2


def draw_lengths(key, part):
    first_key, second_key = jax.random.split(key)
    drawn = jax.random.randint(first_key, (SEQS,), LEN // 2, LEN + 1)
    chosen = jax.random.randint(second_key, (), 0, SEQS)
    return jnp.where(jnp.arange(SEQS) == chosen, LEN, drawn).astype(jnp.int32)


def shard_levels(key, shape, cuts, low, top_value):
    level = 1.0
    for dim, parts in cuts:
        heights = jax.random.uniform(jax.random.fold_in(jax.random.fold_in(key, 6), dim), (parts,), jnp.float32, low / len(cuts), top_value / len(cuts))
        level = level * jnp.repeat(jnp.exp(heights), shape[dim] // parts).reshape((-1,) + (1,) * (len(shape) - 1 - dim))
    return level


def normal_values(own_key, dims, scale, most, cuts=(), kind=jnp.bfloat16):
    array = jax.random.normal(own_key, dims, jnp.float32) * scale
    if len(cuts) > 0:
        array = shard_levels(own_key, dims, cuts, -0.22, 0.18) * array
    return jnp.clip(array, min=-most, max=most).astype(kind)


def setup_inputs(seed: int = 0) -> dict:
    splits = jax.random.split(jax.random.key(seed), 15)
    return {
        "tokens": normal_values(splits[0], (SEQS, LEN, D), 1.0, 6.0, ((0, 2), (1, 4))),
        "time_steps": jax.random.randint(splits[1], (SEQS,), 0, TSTEPS).astype(jnp.int32),
        "lengths": draw_lengths(jax.random.fold_in(splits[14], 71), 0),
        "time_table": normal_values(splits[3], (TSTEPS, D), 0.5, 3.0, ((1, 2),)),
        "norm_gains": jnp.clip(1.0 + 0.1 * jax.random.normal(splits[4], (2, D), jnp.float32), 0.5, 1.5).astype(jnp.bfloat16),
        "norm_biases": normal_values(splits[5], (2, D), 0.2, 1.0, ((1, 2),)),
        "w_qkv": normal_values(splits[6], (3, D, D), (D // 2) ** -0.5, 0.3125, ((1, 2), (2, 4))),
        "b_qv": normal_values(splits[7], (2, D), 0.02, 0.099609375, ((1, 4),)),
        "w_out": normal_values(splits[8], (D, D), (D // 2) ** -0.5, 0.3125, ((0, 4), (1, 2))),
        "out_biases": normal_values(splits[9], (2, D), 0.25, 1.25, ((1, 2),)),
        "w_up": normal_values(splits[10], (D, FF), D ** -0.5, 0.21875, ((0, 2), (1, 4))),
        "b_up": normal_values(splits[11], (FF,), 0.2, 1.0, ((0, 4),)),
        "w_down": normal_values(splits[12], (FF, D), FF ** -0.5, 0.109375, ((0, 4), (1, 2))),
        "cotangent": normal_values(splits[13], (SEQS, LEN, D), 1.0, 6.0, ((0, 2), (1, 4))),
    }


norm_eps = 1e-05
highest = lax.Precision.HIGHEST

@jax.custom_vjp
def low(v):
    return lax.optimization_barrier(v.astype(jnp.bfloat16)).astype(jnp.float32)

@jax.custom_vjp
def low_back(v):
    return v

def low_keep(v):
    return (low(v), None)

def low_pass(kept, grad):
    return (grad,)

def back_keep(v):
    return (v, None)

def back_low(kept, grad):
    return (low(grad),)
low.defvjp(low_keep, low_pass)
low_back.defvjp(back_keep, back_low)

def matmul(left, right):
    return jnp.dot(left, right, precision=highest, preferred_element_type=jnp.float32)

def normalize(values, gain_row, shift_row):
    center = values - lax.optimization_barrier(jnp.mean(values, axis=-1, keepdims=True))
    spread = lax.optimization_barrier(jnp.mean(center * center, axis=-1, keepdims=True))
    return center * lax.rsqrt(spread + norm_eps) * gain_row + shift_row

def attend_block(query_block, keys_all, values_all, key_mask):
    scores = jnp.einsum('qhe,khe->hqk', query_block, keys_all, precision=highest) * HEAD ** (-0.5)
    scores = low_back(scores)
    scores = jnp.where(key_mask[None, None, :], scores, -1e+30)
    weights = low(jax.nn.softmax(scores, axis=-1))
    return jnp.einsum('hqk,khe->qhe', weights, values_all, precision=highest)

def attend_sequence(inputs):
    queries, keys_all, values_all, length = inputs
    key_mask = jnp.arange(LEN) < length
    block_rows = min(512, LEN)
    query_blocks = queries.reshape(LEN // block_rows, block_rows, HEADS, HEAD)
    runner = jax.checkpoint(lambda query_block: attend_block(query_block, keys_all, values_all, key_mask))
    return lax.map(runner, query_blocks).reshape(LEN, HEADS, HEAD)

def forward(params, tokens, time_steps, lengths):
    time_table, norm_gains, norm_biases, w_qkv, b_qv, w_out, out_biases, w_up, b_up, w_down = params
    start_rows = (tokens + time_table[time_steps][:, None, :]).reshape(SEQS * LEN, D)
    normed = low(normalize(start_rows, norm_gains[0], norm_biases[0]))
    queries = low_back(low(matmul(normed, w_qkv[0]) + b_qv[0]))
    keys_all = low_back(low(matmul(normed, w_qkv[1])))
    values_all = low_back(low(matmul(normed, w_qkv[2]) + b_qv[1]))

    def shaped(field_rows):
        return field_rows.reshape(SEQS, LEN, HEADS, HEAD)
    attended = lax.map(jax.checkpoint(attend_sequence), (shaped(queries), shaped(keys_all), shaped(values_all), lengths))
    attended = low_back(low(attended.reshape(SEQS * LEN, D)))
    middle = start_rows + low_back(matmul(attended, w_out) + out_biases[0])
    second = low(normalize(middle, norm_gains[1], norm_biases[1]))
    hidden = low_back(matmul(second, w_up) + b_up)
    activated = low(jax.nn.gelu(hidden, approximate=False))
    result = middle + low_back(matmul(activated, w_down) + out_biases[1])
    return result.reshape(SEQS, LEN, D)

def reference(tokens, time_steps, lengths, time_table, norm_gains, norm_biases, w_qkv, b_qv, w_out, out_biases, w_up, b_up, w_down, cotangent):
    params = tuple((argument.astype(jnp.float32) for argument in (time_table, norm_gains, norm_biases, w_qkv, b_qv, w_out, out_biases, w_up, b_up, w_down)))
    result, pull_back = jax.vjp(lambda weights, inputs: forward(weights, inputs, time_steps, lengths), params, tokens.astype(jnp.float32))
    valid = (jnp.arange(LEN)[None, :] < lengths[:, None]).astype(jnp.float32)
    grad_params, grad_tokens = pull_back(cotangent.astype(jnp.float32) * valid[:, :, None])
    return (result.astype(jnp.bfloat16), grad_tokens, grad_params[0], grad_params[1], grad_params[2], grad_params[3], grad_params[4], grad_params[5], grad_params[6], grad_params[7], grad_params[8], grad_params[9])
```

```python
import functools

import jax
import jax.numpy as jnp
from jax import lax
from jax.experimental import pallas as pl
from jax.experimental.pallas import tpu as pltpu
from jax.sharding import PartitionSpec as P

HEAD = 64
norm_eps = 1e-05
NT = (((1,), (1,)), ((), ()))
NN = (((1,), (0,)), ((), ()))
f32 = jnp.float32
bf16 = jnp.bfloat16
KERNEL_VMEM = 60 * 2**20


def dot(a, b, dims=NN):
    return lax.dot_general(a, b, dims, preferred_element_type=f32)


def attend_body(heads, piece, blocks, first, last, q_ref, *refs):
    kv_refs, bias_refs, refs = refs[:blocks], refs[blocks : 2 * blocks], refs[2 * blocks :]
    if first:
        out_ref, stat_ref, score_ref = refs
    else:
        part_ref, old_ref, out_ref, stat_ref, score_ref = refs
    rows = q_ref.shape[0]
    length = kv_refs[0].shape[1]
    width = heads * HEAD
    pieces = [(b, c) for b in range(blocks) for c in range(0, length, piece)]
    stats = []
    for h in range(heads):
        cols = slice(h * HEAD, (h + 1) * HEAD)
        vals = slice(width + h * HEAD, width + (h + 1) * HEAD)
        q = q_ref[:, cols]
        peak = None
        for b, c in pieces:
            scores = dot(q, kv_refs[b][cols, c : c + piece]) + bias_refs[b][:, c : c + piece]
            score_ref[h, :, b * length + c : b * length + c + piece] = scores
            for j in range(0, piece, 128):
                part = scores[:, j : j + 128]
                peak = part if peak is None else jnp.maximum(peak, part)
        peak = jnp.max(peak, axis=1, keepdims=True)
        if not first:
            old_peak = old_ref[:, h : h + 1]
            peak = jnp.maximum(peak, old_peak)
        total, summed = None, None
        for b, c in pieces:
            weights = jnp.exp(score_ref[h, :, b * length + c : b * length + c + piece] - peak)
            for j in range(0, piece, 128):
                part = weights[:, j : j + 128]
                total = part if total is None else total + part
            part = dot(weights.astype(bf16), kv_refs[b][vals, c : c + piece], NT)
            summed = part if summed is None else summed + part
        total = jnp.sum(total, axis=1, keepdims=True)
        if not first:
            shrink = jnp.exp(old_peak - peak)
            total = total + old_ref[:, 8 + h : 9 + h] * shrink
            summed = summed + part_ref[:, cols] * shrink
        if last:
            summed = summed / total
        stats.append((peak, total))
        out_ref[:, cols] = summed
    lane = lax.broadcasted_iota(jnp.int32, (rows, 128), 1)
    packed = jnp.zeros((rows, 128), f32)
    for h, (peak, total) in enumerate(stats):
        if last:
            packed = jnp.where(lane == h, peak + jnp.log(total), packed)
        else:
            packed = jnp.where(lane == h, peak, packed)
            packed = jnp.where(lane == 8 + h, total, packed)
    stat_ref[...] = packed


def row_spec(rows, width):
    return pl.BlockSpec((rows, width), lambda i: (i, 0))


def whole_spec(array):
    zeros = (0,) * array.ndim
    return pl.BlockSpec(array.shape, lambda i: zeros)


def attend(queries, kvs, biases, carry, last, rows=256, piece=512):
    count, width = queries.shape
    length = kvs[0].shape[1]
    heads = width // HEAD
    keys = length * len(kvs)
    args = [queries, *kvs, *biases]
    specs = [row_spec(rows, width)] + [whole_spec(a) for a in args[1:]]
    if carry is not None:
        args += list(carry)
        specs += [row_spec(rows, width), row_spec(rows, 128)]
    return pl.pallas_call(
        functools.partial(attend_body, heads, piece, len(kvs), carry is None, last),
        grid=(count // rows,),
        in_specs=specs,
        out_specs=[row_spec(rows, width), row_spec(rows, 128)],
        out_shape=[
            jax.ShapeDtypeStruct((count, width), f32),
            jax.ShapeDtypeStruct((count, 128), f32),
        ],
        scratch_shapes=[pltpu.VMEM((heads, rows, keys), f32)],
        cost_estimate=pl.CostEstimate(
            flops=16 * count * keys * width,
            bytes_accessed=count * width * 6 + keys * width * 4,
            transcendentals=count * keys * heads,
        ),
        compiler_params=pltpu.CompilerParams(vmem_limit_bytes=KERNEL_VMEM),
        name="attend",
    )(*args)


def attend_back_body(heads, piece, blocks, first, q_ref, do_ref, att_ref, log_ref, *refs):
    kv_refs, bias_refs, refs = refs[:blocks], refs[blocks : 2 * blocks], refs[2 * blocks :]
    if not first:
        part_ref, refs = refs[0], refs[1:]
    dq_ref, dkv_refs, sum_refs = refs[0], refs[1 : 1 + blocks], refs[1 + blocks :]
    step = pl.program_id(0)
    length = kv_refs[0].shape[1]
    width = heads * HEAD

    @pl.when(step == 0)
    def _():
        for sum_ref in sum_refs:
            sum_ref[...] = jnp.zeros_like(sum_ref)

    q, do = q_ref[...], do_ref[...]
    q_t, do_t = q.T, do.T
    product = do.astype(f32) * att_ref[...]
    for h in range(heads):
        cols = slice(h * HEAD, (h + 1) * HEAD)
        vals = slice(width + h * HEAD, width + (h + 1) * HEAD)
        delta = jnp.sum(product[:, cols], axis=1, keepdims=True)
        log_total = log_ref[:, h : h + 1]
        dq = None
        for b in range(blocks):
            for c in range(0, length, piece):
                span = slice(c, c + piece)
                scores = dot(q[:, cols], kv_refs[b][cols, span]) + bias_refs[b][:, span]
                probs = jnp.exp(scores - log_total)
                grads = dot(do[:, cols], kv_refs[b][vals, span])
                score_grad = (probs * (grads - delta)).astype(bf16)
                part = dot(score_grad, kv_refs[b][cols, span], NT)
                dq = part if dq is None else dq + part
                sum_refs[b][cols, span] += dot(q_t[cols, :], score_grad)
                sum_refs[b][vals, span] += dot(do_t[cols, :], probs.astype(bf16))
        dq = dq * HEAD ** (-0.5)
        if not first:
            dq = dq + part_ref[:, cols]
        dq_ref[:, cols] = dq.astype(dq_ref.dtype)

    @pl.when(step == pl.num_programs(0) - 1)
    def _():
        for dkv_ref, sum_ref in zip(dkv_refs, sum_refs):
            dkv_ref[...] = sum_ref[...].astype(dkv_ref.dtype)


def attend_back(queries, do, att, log_total, kvs, biases, part, rows=512, piece=1024):
    count, width = queries.shape
    length = kvs[0].shape[1]
    heads = width // HEAD
    keys = length * len(kvs)
    args = [queries, do, att, log_total, *kvs, *biases]
    specs = [row_spec(rows, width)] * 3 + [row_spec(rows, 128)]
    specs += [whole_spec(a) for a in args[4:]]
    if part is not None:
        args.append(part)
        specs.append(row_spec(rows, width))
    return pl.pallas_call(
        functools.partial(attend_back_body, heads, piece, len(kvs), part is None),
        grid=(count // rows,),
        in_specs=specs,
        out_specs=[row_spec(rows, width)] + [whole_spec(kv) for kv in kvs],
        out_shape=[jax.ShapeDtypeStruct((count, width), f32 if part is None else bf16)]
        + [jax.ShapeDtypeStruct(kv.shape, bf16) for kv in kvs],
        scratch_shapes=[pltpu.VMEM(kv.shape, f32) for kv in kvs],
        cost_estimate=pl.CostEstimate(
            flops=40 * count * keys * width,
            bytes_accessed=count * width * 12 + keys * width * 8,
            transcendentals=count * keys * heads,
        ),
        compiler_params=pltpu.CompilerParams(vmem_limit_bytes=KERNEL_VMEM),
        name="attend_back",
    )(*args)


def middle_body(
    num_ref, att_ref, tok_ref, emb_ref, par_ref, bup_ref, cot_ref, wout_ref, w_ref,
    layer_ref, back_ref, do_ref, grad_ref, vec_ref, bvec_ref,
    mid_ref, sec_ref, sect_ref, upl_ref, uplt_ref, mlp_ref, sback_ref,
):
    step = pl.program_id(0)
    tps, rows, width = att_ref.shape
    model = tok_ref.shape[1]
    wide = w_ref.shape[2] // 2

    @pl.when(step == 0)
    def _():
        start = tok_ref[...].astype(f32) + emb_ref[...]
        attn = None
        for t in range(tps):
            part = dot(att_ref[t], wout_ref[t][:, :width], NT)
            attn = part if attn is None else attn + part
        middle = start + attn + par_ref[2:3, :]
        mid_ref[...] = middle
        center = middle - jnp.mean(middle, axis=1, keepdims=True)
        scale = lax.rsqrt(jnp.mean(center * center, axis=1, keepdims=True) + norm_eps)
        second = (center * scale * par_ref[0:1, :] + par_ref[1:2, :]).astype(bf16)
        sec_ref[...] = second
        sect_ref[...] = second.T
        place = num_ref[0] + lax.broadcasted_iota(jnp.int32, (rows, model), 0)
        upstream = jnp.where(place < num_ref[1], cot_ref[...].astype(f32), 0.0)
        low = upstream.astype(bf16)
        upl_ref[...] = low
        uplt_ref[...] = low.T
        mlp_ref[...] = jnp.zeros_like(mlp_ref)
        sback_ref[...] = jnp.zeros_like(sback_ref)

    w_up, w_down = w_ref[0, :, :wide], w_ref[0, :, wide:]
    hidden = dot(sec_ref[...], w_up) + bup_ref[pl.ds(step, 1), :]
    half = 0.5 * (1.0 + lax.erf(hidden * (0.5**0.5)))
    activated = (hidden * half).astype(bf16)
    mlp_ref[...] += dot(activated, w_down, NT)
    act_back = dot(upl_ref[...], w_down)
    slope = half + hidden * (jnp.exp(-0.5 * hidden * hidden) * 0.3989422804014327)
    hidden_back = (act_back * slope).astype(bf16)
    sback_ref[...] += dot(hidden_back, w_up, NT)
    bvec_ref[pl.ds(step, 1), :] = jnp.sum(hidden_back.astype(f32), axis=0, keepdims=True)
    grad_ref[pl.ds(step, 1), :, :wide] = dot(sect_ref[...], hidden_back).astype(bf16)[None]
    grad_ref[pl.ds(step, 1), :, wide : 2 * wide] = dot(uplt_ref[...], activated).astype(bf16)[None]

    @pl.when(step == pl.num_programs(0) - 1)
    def _():
        middle = mid_ref[...]
        layer_ref[...] = (middle + mlp_ref[...] + par_ref[3:4, :]).astype(bf16)
        center = middle - jnp.mean(middle, axis=1, keepdims=True)
        scale = lax.rsqrt(jnp.mean(center * center, axis=1, keepdims=True) + norm_eps)
        n = center * scale
        e = sback_ref[...]
        eg = e * par_ref[0:1, :]
        norm = scale * (
            eg
            - jnp.mean(eg, axis=1, keepdims=True)
            - n * jnp.mean(eg * n, axis=1, keepdims=True)
        )
        upstream = upl_ref[...].astype(f32)
        back = upstream + norm
        back_ref[...] = back
        low = back.astype(bf16)
        low_t = low.T
        for t in range(tps):
            do_ref[t] = dot(low, wout_ref[t][:, :width]).astype(bf16)
            grad_ref[t, :, 2 * wide : 2 * wide + width] = dot(low_t, att_ref[t]).astype(bf16)
        vec_ref[0:1, :] = jnp.sum(e * n, axis=0, keepdims=True)
        vec_ref[1:2, :] = jnp.sum(e, axis=0, keepdims=True)
        vec_ref[2:3, :] = jnp.sum(low.astype(f32), axis=0, keepdims=True)
        vec_ref[3:4, :] = jnp.sum(upstream, axis=0, keepdims=True)
        vec_ref[4:8, :] = jnp.zeros((4, model), f32)


def middle_part(numbers, att, tokens, embedded, params, b_up, cotangent, weights):
    tps, rows, width = att.shape
    model = tokens.shape[1]
    packed = weights.shape[2]
    wide = b_up.shape[1]
    fixed = lambda shape: pl.BlockSpec(shape, lambda i, n: (0,) * len(shape))
    mine = pl.BlockSpec((rows, model), lambda i, n: (n[2], 0))
    spare = packed - 2 * wide
    return pl.pallas_call(
        middle_body,
        grid_spec=pltpu.PrefetchScalarGridSpec(
            num_scalar_prefetch=1,
            grid=(tps,),
            in_specs=[
                fixed(att.shape),
                mine,
                fixed(embedded.shape),
                fixed(params.shape),
                fixed(b_up.shape),
                mine,
                pl.BlockSpec((tps, model, spare), lambda i, n: (0, 0, 2 * wide // spare)),
                pl.BlockSpec((1, model, 2 * wide), lambda i, n: (i, 0, 0)),
            ],
            out_specs=[
                fixed((rows, model)),
                fixed((rows, model)),
                fixed(att.shape),
                fixed(weights.shape),
                fixed((8, model)),
                fixed(b_up.shape),
            ],
            scratch_shapes=[
                pltpu.VMEM((rows, model), f32),
                pltpu.VMEM((rows, model), bf16),
                pltpu.VMEM((model, rows), bf16),
                pltpu.VMEM((rows, model), bf16),
                pltpu.VMEM((model, rows), bf16),
                pltpu.VMEM((rows, model), f32),
                pltpu.VMEM((rows, model), f32),
            ],
        ),
        out_shape=[
            jax.ShapeDtypeStruct((rows, model), bf16),
            jax.ShapeDtypeStruct((rows, model), f32),
            jax.ShapeDtypeStruct(att.shape, bf16),
            jax.ShapeDtypeStruct(weights.shape, bf16),
            jax.ShapeDtypeStruct((8, model), f32),
            jax.ShapeDtypeStruct(b_up.shape, f32),
        ],
        cost_estimate=pl.CostEstimate(
            flops=12 * rows * model * wide * tps,
            bytes_accessed=2 * weights.size * 2,
            transcendentals=2 * rows * wide * tps,
        ),
        compiler_params=pltpu.CompilerParams(vmem_limit_bytes=KERNEL_VMEM),
        name="middle",
    )(numbers, att, tokens, embedded, params, b_up, cotangent, weights, weights)


def shift(value, axis, size, by):
    return lax.ppermute(value, axis, [(i, (i + by) % size) for i in range(size)])


def flip(value, axis, size, bit):
    return lax.ppermute(value, axis, [(i, i ^ bit) for i in range(size)])


def swap_rows(value, tps):
    return lax.all_to_all(value, "tp", 0, 0, tiled=True)


def on_device(
    dps, ctxs, tps,
    tokens, time_steps, lengths, time_table, norm_gains, norm_biases, w_qkv, b_qv, w_out,
    out_biases, w_up, b_up, w_down, cotangent,
):
    _, row_count, model = tokens.shape
    local = b_qv.shape[1]
    heads = local // HEAD
    wide = b_up.shape[0]
    part = w_up.shape[0]
    steps_in_table = time_table.shape[0]
    rows = row_count // tps
    dp, ctx, tp = lax.axis_index("dp"), lax.axis_index("ctx"), lax.axis_index("tp")

    all_steps = lax.all_gather(time_steps, "dp", tiled=True)
    small = jnp.concatenate((norm_gains, norm_biases, out_biases, time_table[all_steps]))
    small = lax.all_gather(small, "dp", axis=1, tiled=True).astype(f32)
    embedded = lax.dynamic_slice_in_dim(small, 6 + dp, 1, 0)
    gain_first, shift_first = small[0:1], small[2:3]
    params = jnp.stack(
        (small[1], small[3], small[4], small[5], small[1], small[1], small[1], small[1])
    )

    qkv_mine = jnp.concatenate((w_qkv[0], w_qkv[1], w_qkv[2]), axis=1)
    qkv_full = lax.all_gather(qkv_mine, "dp", axis=0, tiled=True)
    slab = part // ctxs
    spare = -(-local // 128) * 128
    piece = jnp.concatenate(
        (
            lax.dynamic_slice_in_dim(w_up, ctx * slab, slab, 0),
            lax.dynamic_slice_in_dim(w_down, ctx * slab, slab, 1).T,
            jnp.pad(
                lax.dynamic_slice_in_dim(w_out, ctx * slab, slab, 1).T,
                ((0, 0), (0, spare - local)),
            ),
        ),
        axis=1,
    )
    weights = lax.all_gather(piece, ("tp", "dp", "ctx"), axis=0, tiled=True)
    weights = weights.reshape(tps, model, 2 * wide + spare)

    flat = tokens.reshape(row_count, model)
    start = flat.astype(f32) + embedded
    center = start - jnp.mean(start, axis=1, keepdims=True)
    scale = lax.rsqrt(jnp.mean(center * center, axis=1, keepdims=True) + norm_eps)
    normed = (center * scale * gain_first + shift_first).astype(bf16)
    bias = b_qv.astype(f32)
    kv_bias = jnp.concatenate((jnp.zeros((local,), f32), bias[1]))[:, None]
    kv = lax.dot_general(
        qkv_full[:, local:], normed, (((0,), (1,)), ((), ())), preferred_element_type=f32
    )
    kv = (kv + kv_bias).astype(bf16)
    queries = (dot(normed, qkv_full[:, :local]) + bias[0]).astype(bf16) * bf16(HEAD**-0.5)

    place = jnp.arange(row_count)[None, :]

    def key_bias(owner):
        return jnp.where(owner * row_count + place < lengths[0], 0.0, -1e30).astype(f32)

    biases = [key_bias(ctx ^ b) for b in range(4)]
    kv_1 = flip(kv, "ctx", ctxs, 1)
    kv_2 = flip(kv, "ctx", ctxs, 2)
    kv_3 = flip(kv_2, "ctx", ctxs, 1)
    carry = attend(queries, (kv, kv_1), biases[:2], None, False)
    attended, log_total = attend(queries, (kv_2, kv_3), biases[2:], carry, True)

    swapped = swap_rows(attended.astype(bf16).reshape(tps, rows, local), tps)
    numbers = jnp.stack((ctx * row_count + tp * rows, lengths[0], tp)).astype(jnp.int32)
    layer_rows, middle_back, output_back, grad_packed, vectors, grad_b_up = middle_part(
        numbers,
        swapped,
        flat,
        embedded,
        params,
        lax.all_gather(b_up.astype(bf16), "tp").astype(f32),
        cotangent.reshape(row_count, model),
        weights,
    )
    layer_out = lax.all_gather(layer_rows, "tp", axis=0, tiled=True)
    output_back = swap_rows(output_back, tps).reshape(row_count, local)

    grad_packed = lax.psum_scatter(
        grad_packed.reshape(tps * model, -1), ("tp", "dp", "ctx"), scatter_dimension=0, tiled=True
    )
    grad_packed = lax.all_gather(grad_packed, "ctx", axis=0, tiled=True).astype(f32)
    grad_w_up = grad_packed[:, :wide]
    grad_w_down = grad_packed[:, wide : 2 * wide].T
    grad_w_out = grad_packed[:, 2 * wide : 2 * wide + local].T

    dq, dkv_2, dkv_3 = attend_back(
        queries, output_back, attended, log_total, (kv_2, kv_3), biases[2:], None
    )
    far = (dkv_2.astype(f32) + flip(dkv_3, "ctx", ctxs, 1).astype(f32)).astype(bf16)
    far = flip(far, "ctx", ctxs, 2)
    dq, dkv_0, dkv_1 = attend_back(
        queries, output_back, attended, log_total, (kv, kv_1), biases[:2], dq
    )
    near = flip(dkv_1, "ctx", ctxs, 1)
    dkv = (dkv_0.astype(f32) + near.astype(f32) + far.astype(f32)).astype(bf16)

    back = dot(dq, qkv_full[:, :local], NT) + lax.dot_general(
        dkv, qkv_full[:, local:], (((0,), (1,)), ((), ())), preferred_element_type=f32
    )
    back = swap_rows(back.astype(bf16).reshape(tps, rows, model), tps)
    grad_qkv = jnp.concatenate(
        (
            lax.dot_general(normed, dq, (((0,), (0,)), ((), ())), preferred_element_type=f32),
            lax.dot_general(normed, dkv, (((0,), (1,)), ((), ())), preferred_element_type=f32),
        ),
        axis=1,
    ).astype(bf16)
    grad_qkv = lax.psum_scatter(grad_qkv, ("dp", "ctx"), scatter_dimension=0, tiled=True)
    grad_qkv = lax.all_gather(grad_qkv, "ctx", axis=0, tiled=True).astype(f32)
    grad_w_qkv = jnp.stack([grad_qkv[:, i * local : (i + 1) * local] for i in range(3)])

    e = jnp.sum(back.astype(f32), axis=0)
    mine = lax.dynamic_slice_in_dim(flat, tp * rows, rows, 0).astype(f32) + embedded
    center = mine - jnp.mean(mine, axis=1, keepdims=True)
    scale = lax.rsqrt(jnp.mean(center * center, axis=1, keepdims=True) + norm_eps)
    n = center * scale
    eg = e * gain_first
    start_norm = scale * (
        eg - jnp.mean(eg, axis=1, keepdims=True) - n * jnp.mean(eg * n, axis=1, keepdims=True)
    )
    grad_rows = middle_back + start_norm
    low_rows = grad_rows.astype(bf16)
    grad_tokens = jnp.zeros((row_count, model), f32)
    for by in range(tps):
        moved = low_rows if by == 0 else shift(low_rows, "tp", tps, by)
        grad_tokens = lax.dynamic_update_slice_in_dim(
            grad_tokens, moved.astype(f32), ((tp - by) % tps) * rows, 0
        )

    token_sums = jnp.zeros((dps, model), f32)
    token_sums = lax.dynamic_update_slice_in_dim(
        token_sums, jnp.sum(grad_rows, axis=0, keepdims=True), dp, 0
    )
    qv_sums = jnp.concatenate(
        (jnp.sum(dq.astype(f32), axis=0), jnp.sum(dkv[local:].astype(f32), axis=1))
    )
    qv_slots = jnp.zeros((tps, 2 * local), f32)
    qv_slots = lax.dynamic_update_slice_in_dim(qv_slots, qv_sums[None], tp, 0)
    sums = jnp.concatenate(
        (
            vectors[:4],
            jnp.sum(e * n, axis=0, keepdims=True),
            jnp.sum(e, axis=0, keepdims=True),
            token_sums,
            grad_b_up.reshape(-1, model),
            qv_slots.reshape(-1, model),
        )
    )
    sums = lax.psum(sums, ("dp", "ctx", "tp"))
    own = lax.dynamic_slice_in_dim(sums, dp * part, part, 1)
    grad_gains = jnp.stack((own[4], own[0]))
    grad_shifts = jnp.stack((own[5], own[1]))
    grad_out_biases = jnp.stack((own[2], own[3]))
    at = 6 + dps
    b_rows = grad_b_up.size // model
    grad_b_up = lax.dynamic_slice_in_dim(
        sums[at : at + b_rows].reshape(-1), tp * wide, wide, 0
    )
    grad_b_qv = lax.dynamic_index_in_dim(
        sums[at + b_rows :].reshape(tps, 2, local), tp, 0, False
    )
    step_rows = jnp.arange(steps_in_table)[:, None]
    grad_table = jnp.zeros((steps_in_table, part), f32)
    for s in range(dps):
        grad_table = grad_table + jnp.where(step_rows == all_steps[s], own[6 + s][None], 0.0)
    return (
        layer_out[None],
        grad_tokens[None],
        grad_table,
        grad_gains,
        grad_shifts,
        grad_w_qkv,
        grad_b_qv,
        grad_w_out,
        grad_out_biases,
        grad_w_up,
        grad_b_up,
        grad_w_down,
    )


def solution(mesh):
    in_specs = (
        P("dp", "ctx", None),
        P("dp"),
        P("dp"),
        P(None, "dp"),
        P(None, "dp"),
        P(None, "dp"),
        P(None, "dp", "tp"),
        P(None, "tp"),
        P("tp", "dp"),
        P(None, "dp"),
        P("dp", "tp"),
        P("tp"),
        P("tp", "dp"),
        P("dp", "ctx", None),
    )
    out_specs = (
        P("dp", "ctx", None),
        P("dp", "ctx", None),
        P(None, "dp"),
        P(None, "dp"),
        P(None, "dp"),
        P(None, "dp", "tp"),
        P(None, "tp"),
        P("tp", "dp"),
        P(None, "dp"),
        P("dp", "tp"),
        P("tp"),
        P("tp", "dp"),
    )
    sizes = (mesh.shape["dp"], mesh.shape["ctx"], mesh.shape["tp"])
    return jax.shard_map(
        functools.partial(on_device, *sizes),
        mesh=mesh,
        in_specs=in_specs,
        out_specs=out_specs,
        check_vma=False,
    )
```

```python
import functools

import jax
import jax.numpy as jnp
from jax import lax
from jax.experimental import pallas as pl
from jax.experimental.pallas import tpu as pltpu
from jax.sharding import PartitionSpec as P

HEAD = 64
norm_eps = 1e-05
NT = (((1,), (1,)), ((), ()))
NN = (((1,), (0,)), ((), ()))
f32 = jnp.float32
bf16 = jnp.bfloat16
KERNEL_VMEM = 60 * 2**20


def dot(a, b, dims=NN):
    return lax.dot_general(a, b, dims, preferred_element_type=f32)


def attend_body(heads, piece, blocks, first, last, q_ref, *refs):
    kv_refs, bias_refs, refs = refs[:blocks], refs[blocks : 2 * blocks], refs[2 * blocks :]
    if not first:
        (part_ref, old_ref), refs = refs[:2], refs[2:]
    out_ref, stat_ref, score_ref = refs[0], refs[1], refs[-1]
    rows = q_ref.shape[0]
    length = kv_refs[0].shape[1]
    width = heads * HEAD
    pieces = [(b, c) for b in range(blocks) for c in range(0, length, piece)]
    stats = []
    for h in range(heads):
        cols = slice(h * HEAD, (h + 1) * HEAD)
        vals = slice(width + h * HEAD, width + (h + 1) * HEAD)
        q = q_ref[:, cols]
        peak = None
        for b, c in pieces:
            scores = dot(q, kv_refs[b][cols, c : c + piece]) + bias_refs[b][:, c : c + piece]
            score_ref[h, :, b * length + c : b * length + c + piece] = scores
            for j in range(0, piece, 128):
                part = scores[:, j : j + 128]
                peak = part if peak is None else jnp.maximum(peak, part)
        peak = jnp.max(peak, axis=1, keepdims=True)
        if not first:
            old_peak = old_ref[:, h : h + 1]
            peak = jnp.maximum(peak, old_peak)
        total, summed = None, None
        for b, c in pieces:
            weights = jnp.exp(score_ref[h, :, b * length + c : b * length + c + piece] - peak)
            for j in range(0, piece, 128):
                part = weights[:, j : j + 128]
                total = part if total is None else total + part
            part = dot(weights.astype(bf16), kv_refs[b][vals, c : c + piece], NT)
            summed = part if summed is None else summed + part
        total = jnp.sum(total, axis=1, keepdims=True)
        if not first:
            shrink = jnp.exp(old_peak - peak)
            total = total + old_ref[:, 8 + h : 9 + h] * shrink
            summed = summed + part_ref[:, cols] * shrink
        if last:
            summed = summed / total
        stats.append((peak, total))
        out_ref[:, cols] = summed
        if last:
            refs[2][:, cols] = summed.astype(bf16)
    lane = lax.broadcasted_iota(jnp.int32, (rows, 128), 1)
    packed = jnp.zeros((rows, 128), f32)
    for h, (peak, total) in enumerate(stats):
        if last:
            packed = jnp.where(lane == h, peak + jnp.log(total), packed)
        else:
            packed = jnp.where(lane == h, peak, packed)
            packed = jnp.where(lane == 8 + h, total, packed)
    stat_ref[...] = packed


def row_spec(rows, width):
    return pl.BlockSpec((rows, width), lambda i: (i, 0))


def whole_spec(array):
    zeros = (0,) * array.ndim
    return pl.BlockSpec(array.shape, lambda i: zeros)


def attend(queries, kvs, biases, carry, last, rows=256, piece=512):
    count, width = queries.shape
    length = kvs[0].shape[1]
    heads = width // HEAD
    keys = length * len(kvs)
    args = [queries, *kvs, *biases]
    specs = [row_spec(rows, width)] + [whole_spec(a) for a in args[1:]]
    if carry is not None:
        args += list(carry)
        specs += [row_spec(rows, width), row_spec(rows, 128)]
    return pl.pallas_call(
        functools.partial(attend_body, heads, piece, len(kvs), carry is None, last),
        grid=(count // rows,),
        in_specs=specs,
        out_specs=[row_spec(rows, width), row_spec(rows, 128)]
        + [row_spec(rows, width)] * last,
        out_shape=[
            jax.ShapeDtypeStruct((count, width), f32),
            jax.ShapeDtypeStruct((count, 128), f32),
        ]
        + [jax.ShapeDtypeStruct((count, width), bf16)] * last,
        scratch_shapes=[pltpu.VMEM((heads, rows, keys), f32)],
        cost_estimate=pl.CostEstimate(
            flops=16 * count * keys * width,
            bytes_accessed=count * width * 6 + keys * width * 4,
            transcendentals=count * keys * heads,
        ),
        compiler_params=pltpu.CompilerParams(vmem_limit_bytes=KERNEL_VMEM),
        name="attend",
    )(*args)


def attend_back_body(heads, piece, blocks, first, q_ref, do_ref, att_ref, log_ref, *refs):
    kv_refs, bias_refs, refs = refs[:blocks], refs[blocks : 2 * blocks], refs[2 * blocks :]
    if not first:
        part_ref, refs = refs[0], refs[1:]
    dq_ref, dkv_refs, sum_refs = refs[0], refs[1 : 1 + blocks], refs[1 + blocks :]
    step = pl.program_id(0)
    length = kv_refs[0].shape[1]
    width = heads * HEAD

    @pl.when(step == 0)
    def _():
        for sum_ref in sum_refs:
            sum_ref[...] = jnp.zeros_like(sum_ref)

    q, do = q_ref[...], do_ref[...]
    q_t, do_t = q.T, do.T
    product = do.astype(f32) * att_ref[...]
    for h in range(heads):
        cols = slice(h * HEAD, (h + 1) * HEAD)
        vals = slice(width + h * HEAD, width + (h + 1) * HEAD)
        delta = jnp.sum(product[:, cols], axis=1, keepdims=True)
        log_total = log_ref[:, h : h + 1]
        dq = None
        for b in range(blocks):
            for c in range(0, length, piece):
                span = slice(c, c + piece)
                scores = dot(q[:, cols], kv_refs[b][cols, span]) + bias_refs[b][:, span]
                probs = jnp.exp(scores - log_total)
                grads = dot(do[:, cols], kv_refs[b][vals, span])
                score_grad = (probs * (grads - delta)).astype(bf16)
                part = dot(score_grad, kv_refs[b][cols, span], NT)
                dq = part if dq is None else dq + part
                sum_refs[b][cols, span] += dot(q_t[cols, :], score_grad)
                sum_refs[b][vals, span] += dot(do_t[cols, :], probs.astype(bf16))
        dq = dq * HEAD ** (-0.5)
        if not first:
            dq = dq + part_ref[:, cols]
        dq_ref[:, cols] = dq.astype(dq_ref.dtype)

    @pl.when(step == pl.num_programs(0) - 1)
    def _():
        for dkv_ref, sum_ref in zip(dkv_refs, sum_refs):
            dkv_ref[...] = sum_ref[...].astype(dkv_ref.dtype)


def attend_back(queries, do, att, log_total, kvs, biases, part, rows=512, piece=1024):
    count, width = queries.shape
    length = kvs[0].shape[1]
    heads = width // HEAD
    keys = length * len(kvs)
    args = [queries, do, att, log_total, *kvs, *biases]
    specs = [row_spec(rows, width)] * 3 + [row_spec(rows, 128)]
    specs += [whole_spec(a) for a in args[4:]]
    if part is not None:
        args.append(part)
        specs.append(row_spec(rows, width))
    return pl.pallas_call(
        functools.partial(attend_back_body, heads, piece, len(kvs), part is None),
        grid=(count // rows,),
        in_specs=specs,
        out_specs=[row_spec(rows, width)] + [whole_spec(kv) for kv in kvs],
        out_shape=[jax.ShapeDtypeStruct((count, width), f32 if part is None else bf16)]
        + [jax.ShapeDtypeStruct(kv.shape, bf16) for kv in kvs],
        scratch_shapes=[pltpu.VMEM(kv.shape, f32) for kv in kvs],
        cost_estimate=pl.CostEstimate(
            flops=4 * count * keys * width,
            bytes_accessed=count * width * 12 + keys * width * 8,
            transcendentals=count * keys * heads,
        ),
        compiler_params=pltpu.CompilerParams(vmem_limit_bytes=KERNEL_VMEM),
        name="attend_back",
    )(*args)


def middle_body(
    num_ref, att_ref, tok_ref, emb_ref, par_ref, cot_ref, wout_ref, w_ref,
    layer_ref, back_ref, do_ref, grad_ref, vec_ref, bvec_ref,
    mid_ref, sec_ref, sect_ref, upl_ref, uplt_ref, mlp_ref, sback_ref,
):
    step = pl.program_id(0)
    tps, rows, width = att_ref.shape
    model = tok_ref.shape[1]
    wide = w_ref.shape[2] // 2

    @pl.when(step == 0)
    def _():
        start = tok_ref[...].astype(f32) + emb_ref[...]
        attn = None
        for t in range(tps):
            part = dot(att_ref[t], wout_ref[t][:, :width], NT)
            attn = part if attn is None else attn + part
        middle = start + attn + par_ref[2:3, :]
        mid_ref[...] = middle
        center = middle - jnp.mean(middle, axis=1, keepdims=True)
        scale = lax.rsqrt(jnp.mean(center * center, axis=1, keepdims=True) + norm_eps)
        second = (center * scale * par_ref[0:1, :] + par_ref[1:2, :]).astype(bf16)
        sec_ref[...] = second
        sect_ref[...] = second.T
        place = num_ref[0] + lax.broadcasted_iota(jnp.int32, (rows, model), 0)
        upstream = jnp.where(place < num_ref[1], cot_ref[...].astype(f32), 0.0)
        low = upstream.astype(bf16)
        upl_ref[...] = low
        uplt_ref[...] = low.T
        mlp_ref[...] = jnp.zeros_like(mlp_ref)
        sback_ref[...] = jnp.zeros_like(sback_ref)

    w_up, w_down = w_ref[0, :, :wide], w_ref[0, :, wide:]
    b_up = wout_ref[step][:, width:].astype(f32).T[0:1, :]
    hidden = dot(sec_ref[...], w_up) + b_up
    half = 0.5 * (1.0 + lax.erf(hidden * (0.5**0.5)))
    activated = (hidden * half).astype(bf16)
    mlp_ref[...] += dot(activated, w_down, NT)
    act_back = dot(upl_ref[...], w_down)
    slope = half + hidden * (jnp.exp(-0.5 * hidden * hidden) * 0.3989422804014327)
    hidden_back = (act_back * slope).astype(bf16)
    sback_ref[...] += dot(hidden_back, w_up, NT)
    bvec_ref[pl.ds(step, 1), :] = jnp.sum(hidden_back.astype(f32), axis=0, keepdims=True)
    grad_ref[pl.ds(step, 1), :, :wide] = dot(sect_ref[...], hidden_back).astype(bf16)[None]
    grad_ref[pl.ds(step, 1), :, wide : 2 * wide] = dot(uplt_ref[...], activated).astype(bf16)[None]

    @pl.when(step == pl.num_programs(0) - 1)
    def _():
        middle = mid_ref[...]
        layer_ref[...] = (middle + mlp_ref[...] + par_ref[3:4, :]).astype(bf16)
        center = middle - jnp.mean(middle, axis=1, keepdims=True)
        scale = lax.rsqrt(jnp.mean(center * center, axis=1, keepdims=True) + norm_eps)
        n = center * scale
        e = sback_ref[...]
        eg = e * par_ref[0:1, :]
        norm = scale * (
            eg
            - jnp.mean(eg, axis=1, keepdims=True)
            - n * jnp.mean(eg * n, axis=1, keepdims=True)
        )
        upstream = upl_ref[...].astype(f32)
        back = upstream + norm
        back_ref[...] = back
        low = back.astype(bf16)
        low_t = low.T
        for t in range(tps):
            do_ref[t] = dot(low, wout_ref[t][:, :width]).astype(bf16)
            grad_ref[t, :, 2 * wide : 2 * wide + width] = dot(low_t, att_ref[t]).astype(bf16)
        vec_ref[0:1, :] = jnp.sum(e * n, axis=0, keepdims=True)
        vec_ref[1:2, :] = jnp.sum(e, axis=0, keepdims=True)
        vec_ref[2:3, :] = jnp.sum(low.astype(f32), axis=0, keepdims=True)
        vec_ref[3:4, :] = jnp.sum(upstream, axis=0, keepdims=True)
        vec_ref[4:8, :] = jnp.zeros((4, model), f32)


def middle_part(numbers, att, tokens, embedded, params, cotangent, weights, wide):
    tps, rows, width = att.shape
    model = tokens.shape[1]
    packed = weights.shape[2]
    fixed = lambda shape: pl.BlockSpec(shape, lambda i, n: (0,) * len(shape))
    mine = pl.BlockSpec((rows, model), lambda i, n: (n[2], 0))
    spare = packed - 2 * wide
    return pl.pallas_call(
        middle_body,
        grid_spec=pltpu.PrefetchScalarGridSpec(
            num_scalar_prefetch=1,
            grid=(tps,),
            in_specs=[
                fixed(att.shape),
                mine,
                fixed(embedded.shape),
                fixed(params.shape),
                mine,
                pl.BlockSpec((tps, model, spare), lambda i, n: (0, 0, 2 * wide // spare)),
                pl.BlockSpec((1, model, 2 * wide), lambda i, n: (i, 0, 0)),
            ],
            out_specs=[
                fixed((rows, model)),
                fixed((rows, model)),
                fixed(att.shape),
                fixed(weights.shape),
                fixed((8, model)),
                fixed((tps, wide)),
            ],
            scratch_shapes=[
                pltpu.VMEM((rows, model), f32),
                pltpu.VMEM((rows, model), bf16),
                pltpu.VMEM((model, rows), bf16),
                pltpu.VMEM((rows, model), bf16),
                pltpu.VMEM((model, rows), bf16),
                pltpu.VMEM((rows, model), f32),
                pltpu.VMEM((rows, model), f32),
            ],
        ),
        out_shape=[
            jax.ShapeDtypeStruct((rows, model), bf16),
            jax.ShapeDtypeStruct((rows, model), f32),
            jax.ShapeDtypeStruct(att.shape, bf16),
            jax.ShapeDtypeStruct(weights.shape, bf16),
            jax.ShapeDtypeStruct((8, model), f32),
            jax.ShapeDtypeStruct((tps, wide), f32),
        ],
        cost_estimate=pl.CostEstimate(
            flops=12 * rows * model * wide * tps,
            bytes_accessed=2 * weights.size * 2,
            transcendentals=2 * rows * wide * tps,
        ),
        compiler_params=pltpu.CompilerParams(vmem_limit_bytes=KERNEL_VMEM),
        name="middle",
    )(numbers, att, tokens, embedded, params, cotangent, weights, weights)


def shift(value, axis, size, by):
    return lax.ppermute(value, axis, [(i, (i + by) % size) for i in range(size)])


def flip(value, axis, size, bit):
    return lax.ppermute(value, axis, [(i, i ^ bit) for i in range(size)])


def after(value, *others):
    return lax.optimization_barrier((value, *others))[0]


def swap_rows(value):
    return lax.all_to_all(value, "tp", 0, 0, tiled=True)


def gather_dp(value, dps, axis):
    if dps != 2:
        return lax.all_gather(value, "dp", axis=axis, tiled=True)
    other = flip(value, "dp", 2, 1)
    first = lax.axis_index("dp") == 0
    return jnp.concatenate(
        (jnp.where(first, value, other), jnp.where(first, other, value)), axis=axis
    )


def add_low(*terms):
    total = terms[0].astype(f32)
    for term in terms[1:]:
        total = total + term.astype(f32)
    return total.astype(bf16)


def sum_vectors(value, dps, ctxs, tps):
    for bit in (1, 2):
        value = value + flip(value, "ctx", ctxs, bit)
    if dps == 2:
        value = value + flip(value, "dp", dps, 1)
    else:
        value = lax.psum(value, "dp")
    for bit in (1, 2):
        value = value + flip(value, "tp", tps, bit)
    return value


def reduce_projections(grad, dps, ctxs):
    if dps != 2:
        grad = lax.psum_scatter(grad, ("dp", "ctx"), scatter_dimension=0, tiled=True)
        return lax.all_gather(grad, "ctx", axis=0, tiled=True)
    dp, ctx = lax.axis_index("dp"), lax.axis_index("ctx")
    core, y = ctx % 2, ctx // 2
    size = grad.shape[0] // (dps * 4)
    grad = grad.reshape(2, 2, 2 * size, -1)
    pick = lambda v, i, axis: lax.dynamic_index_in_dim(v, i, axis, False)
    grad = add_low(pick(grad, core, 1), flip(pick(grad, 1 - core, 1), "ctx", ctxs, 1))
    grad = add_low(pick(grad, dp, 0), flip(pick(grad, 1 - dp, 0), "dp", dps, 1))
    grad = grad.reshape(2, size, -1)
    grad = add_low(pick(grad, y, 0), flip(pick(grad, 1 - y, 0), "ctx", ctxs, 2))
    for axis_bit, index in ((2, y), (1, core)):
        other = flip(grad, "ctx", ctxs, axis_bit)
        first = index == 0
        grad = jnp.concatenate((jnp.where(first, grad, other), jnp.where(first, other, grad)))
    return grad


def spread_rows(value, tps):
    copies = swap_rows(jnp.broadcast_to(value[None], (tps, *value.shape)))
    return copies.reshape(tps * value.shape[0], value.shape[1])


def on_device(
    dps, ctxs, tps,
    tokens, time_steps, lengths, time_table, norm_gains, norm_biases, w_qkv, b_qv, w_out,
    out_biases, w_up, b_up, w_down, cotangent,
):
    _, row_count, model = tokens.shape
    local = b_qv.shape[1]
    wide = b_up.shape[0]
    part = w_up.shape[0]
    steps_in_table = time_table.shape[0]
    rows = row_count // tps
    dp, ctx, tp = lax.axis_index("dp"), lax.axis_index("ctx"), lax.axis_index("tp")

    all_steps = gather_dp(time_steps, dps, 0)
    small = jnp.concatenate((norm_gains, norm_biases, out_biases, time_table[all_steps]))
    small = gather_dp(small, dps, 1).astype(f32)
    embedded = lax.dynamic_slice_in_dim(small, 6 + dp, 1, 0)
    gain_first, shift_first = small[0:1], small[2:3]
    params = jnp.stack(
        (small[1], small[3], small[4], small[5], small[1], small[1], small[1], small[1])
    )

    qkv_mine = jnp.concatenate((w_qkv[0], w_qkv[1], w_qkv[2]), axis=1)
    qkv_full = gather_dp(qkv_mine, dps, 0)
    slab = part // ctxs
    spare = -(-(local + 1) // 128) * 128
    piece = jnp.concatenate(
        (
            lax.dynamic_slice_in_dim(w_up, ctx * slab, slab, 0),
            lax.dynamic_slice_in_dim(w_down, ctx * slab, slab, 1).T,
            lax.dynamic_slice_in_dim(w_out, ctx * slab, slab, 1).T,
            lax.dynamic_slice_in_dim(b_up, dp * part + ctx * slab, slab, 0)[:, None],
            jnp.zeros((slab, spare - local - 1), bf16),
        ),
        axis=1,
    )
    weights = lax.all_gather(piece, ("tp", "dp", "ctx"), axis=0, tiled=True)
    weights = weights.reshape(tps, model, 2 * wide + spare)

    flat = tokens.reshape(row_count, model)
    start = flat.astype(f32) + embedded
    center = start - jnp.mean(start, axis=1, keepdims=True)
    scale = lax.rsqrt(jnp.mean(center * center, axis=1, keepdims=True) + norm_eps)
    normed = (center * scale * gain_first + shift_first).astype(bf16)
    bias = b_qv.astype(f32)
    kv_bias = jnp.concatenate((jnp.zeros((local,), f32), bias[1]))[:, None]
    kv = lax.dot_general(
        qkv_full[:, local:], normed, (((0,), (1,)), ((), ())), preferred_element_type=f32
    )
    kv = (kv + kv_bias).astype(bf16)
    queries = (dot(normed, qkv_full[:, :local]) + bias[0]).astype(bf16) * bf16(HEAD**-0.5)

    place = jnp.arange(row_count)[None, :]

    def key_bias(owner):
        return jnp.where(owner * row_count + place < lengths[0], 0.0, -1e30).astype(f32)

    biases = [key_bias(ctx ^ b) for b in range(4)]
    kv_1 = flip(kv, "ctx", ctxs, 1)
    kv_2 = flip(kv, "ctx", ctxs, 2)
    carry = attend(queries, (kv, kv_1), biases[:2], None, False)
    kv_2 = after(kv_2, *carry)
    kv_3 = flip(kv_2, "ctx", ctxs, 1)
    attended, log_total, attended_low = attend(queries, (kv_2, kv_3), biases[2:], carry, True)

    swapped = swap_rows(attended_low.reshape(tps, rows, local))
    numbers = jnp.stack((ctx * row_count + tp * rows, lengths[0], tp)).astype(jnp.int32)
    layer_rows, middle_back, output_back, grad_packed, vectors, grad_b_up = middle_part(
        numbers,
        swapped,
        flat,
        embedded,
        params,
        cotangent.reshape(row_count, model),
        weights,
        wide,
    )
    output_back = swap_rows(output_back).reshape(row_count, local)

    grad_packed = lax.psum_scatter(
        grad_packed.reshape(tps * model, -1), ("tp", "dp", "ctx"), scatter_dimension=0, tiled=True
    )

    layer_out = spread_rows(after(layer_rows, output_back), tps)
    dq, dkv_2, dkv_3 = attend_back(
        queries, output_back, attended, log_total, (kv_2, kv_3), biases[2:], None
    )
    far = add_low(dkv_2, flip(dkv_3, "ctx", ctxs, 1))
    dq = after(dq, far)
    far = flip(far, "ctx", ctxs, 2)
    dq, dkv_0, dkv_1 = attend_back(
        queries, output_back, attended, log_total, (kv, kv_1), biases[:2], dq
    )
    dkv_1, layer_out = lax.optimization_barrier((dkv_1, layer_out))
    near = flip(dkv_1, "ctx", ctxs, 1)
    dkv = add_low(dkv_0, near, far)

    back = dot(dq, qkv_full[:, :local], NT) + lax.dot_general(
        dkv, qkv_full[:, local:], (((0,), (1,)), ((), ())), preferred_element_type=f32
    )
    back = swap_rows(back.astype(bf16).reshape(tps, rows, model))
    grad_qkv = jnp.concatenate(
        (
            lax.dot_general(normed, dq, (((0,), (0,)), ((), ())), preferred_element_type=f32),
            lax.dot_general(normed, dkv, (((0,), (1,)), ((), ())), preferred_element_type=f32),
        ),
        axis=1,
    ).astype(bf16)
    grad_qkv = reduce_projections(grad_qkv, dps, ctxs).astype(f32)
    grad_w_qkv = jnp.stack([grad_qkv[:, i * local : (i + 1) * local] for i in range(3)])

    e = jnp.sum(back.astype(f32), axis=0)
    mine = lax.dynamic_slice_in_dim(flat, tp * rows, rows, 0).astype(f32) + embedded
    center = mine - jnp.mean(mine, axis=1, keepdims=True)
    scale = lax.rsqrt(jnp.mean(center * center, axis=1, keepdims=True) + norm_eps)
    n = center * scale
    eg = e * gain_first
    start_norm = scale * (
        eg - jnp.mean(eg, axis=1, keepdims=True) - n * jnp.mean(eg * n, axis=1, keepdims=True)
    )
    grad_rows = middle_back + start_norm
    grad_tokens = spread_rows(grad_rows.astype(bf16), tps).astype(f32)

    token_sums = jnp.zeros((dps, model), f32)
    token_sums = lax.dynamic_update_slice_in_dim(
        token_sums, jnp.sum(grad_rows, axis=0, keepdims=True), dp, 0
    )
    qv_sums = jnp.concatenate(
        (jnp.sum(dq.astype(f32), axis=0), jnp.sum(dkv[local:].astype(f32), axis=1))
    )
    qv_slots = jnp.zeros((tps, 2 * local), f32)
    qv_slots = lax.dynamic_update_slice_in_dim(qv_slots, qv_sums[None], tp, 0)
    sums = jnp.concatenate(
        (
            vectors[:4],
            jnp.sum(e * n, axis=0, keepdims=True),
            jnp.sum(e, axis=0, keepdims=True),
            token_sums,
            grad_b_up.reshape(-1, model),
            qv_slots.reshape(-1, model),
        )
    )
    grad_packed = after(grad_packed, sums)
    grad_packed = lax.all_gather(grad_packed, "ctx", axis=0, tiled=True).astype(f32)
    grad_w_up = grad_packed[:, :wide]
    grad_w_down = grad_packed[:, wide : 2 * wide].T
    grad_w_out = grad_packed[:, 2 * wide : 2 * wide + local].T
    sums = sum_vectors(sums, dps, ctxs, tps)
    own = lax.dynamic_slice_in_dim(sums, dp * part, part, 1)
    grad_gains = jnp.stack((own[4], own[0]))
    grad_shifts = jnp.stack((own[5], own[1]))
    grad_out_biases = jnp.stack((own[2], own[3]))
    at = 6 + dps
    b_rows = grad_b_up.size // model
    grad_b_up = lax.dynamic_slice_in_dim(
        sums[at : at + b_rows].reshape(-1), tp * wide, wide, 0
    )
    grad_b_qv = lax.dynamic_index_in_dim(
        sums[at + b_rows :].reshape(tps, 2, local), tp, 0, False
    )
    step_rows = jnp.arange(steps_in_table)[:, None]
    grad_table = jnp.zeros((steps_in_table, part), f32)
    for s in range(dps):
        grad_table = grad_table + jnp.where(step_rows == all_steps[s], own[6 + s][None], 0.0)
    return (
        layer_out[None],
        grad_tokens[None],
        grad_table,
        grad_gains,
        grad_shifts,
        grad_w_qkv,
        grad_b_qv,
        grad_w_out,
        grad_out_biases,
        grad_w_up,
        grad_b_up,
        grad_w_down,
    )


def solution(mesh):
    in_specs = (
        P("dp", "ctx", None),
        P("dp"),
        P("dp"),
        P(None, "dp"),
        P(None, "dp"),
        P(None, "dp"),
        P(None, "dp", "tp"),
        P(None, "tp"),
        P("tp", "dp"),
        P(None, "dp"),
        P("dp", "tp"),
        P("tp"),
        P("tp", "dp"),
        P("dp", "ctx", None),
    )
    out_specs = (
        P("dp", "ctx", None),
        P("dp", "ctx", None),
        P(None, "dp"),
        P(None, "dp"),
        P(None, "dp"),
        P(None, "dp", "tp"),
        P(None, "tp"),
        P("tp", "dp"),
        P(None, "dp"),
        P("dp", "tp"),
        P("tp"),
        P("tp", "dp"),
    )
    sizes = (mesh.shape["dp"], mesh.shape["ctx"], mesh.shape["tp"])
    return jax.shard_map(
        functools.partial(on_device, *sizes),
        mesh=mesh,
        in_specs=in_specs,
        out_specs=out_specs,
        check_vma=False,
    )
```

```python
import functools

import jax
import jax.numpy as jnp
from jax import lax
from jax.experimental import pallas as pl
from jax.experimental.pallas import tpu as pltpu
from jax.sharding import PartitionSpec as P

HEAD = 64
norm_eps = 1e-05
NT = (((1,), (1,)), ((), ()))
NN = (((1,), (0,)), ((), ()))
f32 = jnp.float32
bf16 = jnp.bfloat16
KERNEL_VMEM = 60 * 2**20


def dot(a, b, dims=NN):
    return lax.dot_general(a, b, dims, preferred_element_type=f32)


def attend_body(heads, piece, blocks, first, last, q_ref, *refs):
    kv_refs, bias_refs, refs = refs[:blocks], refs[blocks : 2 * blocks], refs[2 * blocks :]
    if not first:
        (part_ref, old_ref), refs = refs[:2], refs[2:]
    out_ref, stat_ref, score_ref = refs[0], refs[1], refs[-1]
    rows = q_ref.shape[0]
    length = kv_refs[0].shape[1]
    width = heads * HEAD
    pieces = [(b, c) for b in range(blocks) for c in range(0, length, piece)]
    stats = []
    for h in range(heads):
        cols = slice(h * HEAD, (h + 1) * HEAD)
        vals = slice(width + h * HEAD, width + (h + 1) * HEAD)
        q = q_ref[:, cols]
        peak = None
        for b, c in pieces:
            scores = dot(q, kv_refs[b][cols, c : c + piece]) + bias_refs[b][:, c : c + piece]
            score_ref[h, :, b * length + c : b * length + c + piece] = scores
            for j in range(0, piece, 128):
                part = scores[:, j : j + 128]
                peak = part if peak is None else jnp.maximum(peak, part)
        peak = jnp.max(peak, axis=1, keepdims=True)
        if not first:
            old_peak = old_ref[:, h : h + 1]
            peak = jnp.maximum(peak, old_peak)
        total, summed = None, None
        for b, c in pieces:
            weights = jnp.exp(score_ref[h, :, b * length + c : b * length + c + piece] - peak)
            for j in range(0, piece, 128):
                part = weights[:, j : j + 128]
                total = part if total is None else total + part
            part = dot(weights.astype(bf16), kv_refs[b][vals, c : c + piece], NT)
            summed = part if summed is None else summed + part
        total = jnp.sum(total, axis=1, keepdims=True)
        if not first:
            shrink = jnp.exp(old_peak - peak)
            total = total + old_ref[:, 8 + h : 9 + h] * shrink
            summed = summed + part_ref[:, cols] * shrink
        if last:
            summed = summed / total
        stats.append((peak, total))
        out_ref[:, cols] = summed
        if last:
            refs[2][:, cols] = summed.astype(bf16)
    lane = lax.broadcasted_iota(jnp.int32, (rows, 128), 1)
    packed = jnp.zeros((rows, 128), f32)
    for h, (peak, total) in enumerate(stats):
        if last:
            packed = jnp.where(lane == h, peak + jnp.log(total), packed)
        else:
            packed = jnp.where(lane == h, peak, packed)
            packed = jnp.where(lane == 8 + h, total, packed)
    stat_ref[...] = packed


def row_spec(rows, width):
    return pl.BlockSpec((rows, width), lambda i: (i, 0))


def whole_spec(array):
    zeros = (0,) * array.ndim
    return pl.BlockSpec(array.shape, lambda i: zeros)


def attend(queries, kvs, biases, carry, last, rows=256, piece=512):
    count, width = queries.shape
    length = kvs[0].shape[1]
    heads = width // HEAD
    keys = length * len(kvs)
    args = [queries, *kvs, *biases]
    specs = [row_spec(rows, width)] + [whole_spec(a) for a in args[1:]]
    if carry is not None:
        args += list(carry)
        specs += [row_spec(rows, width), row_spec(rows, 128)]
    return pl.pallas_call(
        functools.partial(attend_body, heads, piece, len(kvs), carry is None, last),
        grid=(count // rows,),
        in_specs=specs,
        out_specs=[row_spec(rows, width), row_spec(rows, 128)]
        + [row_spec(rows, width)] * last,
        out_shape=[
            jax.ShapeDtypeStruct((count, width), f32),
            jax.ShapeDtypeStruct((count, 128), f32),
        ]
        + [jax.ShapeDtypeStruct((count, width), bf16)] * last,
        scratch_shapes=[pltpu.VMEM((heads, rows, keys), f32)],
        cost_estimate=pl.CostEstimate(
            flops=16 * count * keys * width,
            bytes_accessed=count * width * 6 + keys * width * 4,
            transcendentals=count * keys * heads,
        ),
        compiler_params=pltpu.CompilerParams(vmem_limit_bytes=KERNEL_VMEM),
        name="attend",
    )(*args)


def attend_back_body(heads, piece, blocks, first, q_ref, do_ref, att_ref, log_ref, *refs):
    kv_refs, bias_refs, refs = refs[:blocks], refs[blocks : 2 * blocks], refs[2 * blocks :]
    if not first:
        part_ref, refs = refs[0], refs[1:]
    dq_ref, dkv_refs, sum_refs = refs[0], refs[1 : 1 + blocks], refs[1 + blocks :]
    step = pl.program_id(0)
    length = kv_refs[0].shape[1]
    width = heads * HEAD

    @pl.when(step == 0)
    def _():
        for sum_ref in sum_refs:
            sum_ref[...] = jnp.zeros_like(sum_ref)

    q, do = q_ref[...], do_ref[...]
    q_t, do_t = q.T, do.T
    product = do.astype(f32) * att_ref[...]
    for h in range(heads):
        cols = slice(h * HEAD, (h + 1) * HEAD)
        vals = slice(width + h * HEAD, width + (h + 1) * HEAD)
        delta = jnp.sum(product[:, cols], axis=1, keepdims=True)
        log_total = log_ref[:, h : h + 1]
        dq = None
        for b in range(blocks):
            for c in range(0, length, piece):
                span = slice(c, c + piece)
                scores = dot(q[:, cols], kv_refs[b][cols, span]) + bias_refs[b][:, span]
                probs = jnp.exp(scores - log_total)
                grads = dot(do[:, cols], kv_refs[b][vals, span])
                score_grad = (probs * (grads - delta)).astype(bf16)
                part = dot(score_grad, kv_refs[b][cols, span], NT)
                dq = part if dq is None else dq + part
                sum_refs[b][cols, span] += dot(q_t[cols, :], score_grad)
                sum_refs[b][vals, span] += dot(do_t[cols, :], probs.astype(bf16))
        dq = dq * HEAD ** (-0.5)
        if not first:
            dq = dq + part_ref[:, cols]
        dq_ref[:, cols] = dq.astype(dq_ref.dtype)

    @pl.when(step == pl.num_programs(0) - 1)
    def _():
        for dkv_ref, sum_ref in zip(dkv_refs, sum_refs):
            dkv_ref[...] = sum_ref[...].astype(dkv_ref.dtype)


def attend_back(queries, do, att, log_total, kvs, biases, part, rows=512, piece=1024):
    count, width = queries.shape
    length = kvs[0].shape[1]
    heads = width // HEAD
    keys = length * len(kvs)
    args = [queries, do, att, log_total, *kvs, *biases]
    specs = [row_spec(rows, width)] * 3 + [row_spec(rows, 128)]
    specs += [whole_spec(a) for a in args[4:]]
    if part is not None:
        args.append(part)
        specs.append(row_spec(rows, width))
    return pl.pallas_call(
        functools.partial(attend_back_body, heads, piece, len(kvs), part is None),
        grid=(count // rows,),
        in_specs=specs,
        out_specs=[row_spec(rows, width)] + [whole_spec(kv) for kv in kvs],
        out_shape=[jax.ShapeDtypeStruct((count, width), f32 if part is None else bf16)]
        + [jax.ShapeDtypeStruct(kv.shape, bf16) for kv in kvs],
        scratch_shapes=[pltpu.VMEM(kv.shape, f32) for kv in kvs],
        cost_estimate=pl.CostEstimate(
            flops=4 * count * keys * width,
            bytes_accessed=count * width * 12 + keys * width * 8,
            transcendentals=count * keys * heads,
        ),
        compiler_params=pltpu.CompilerParams(vmem_limit_bytes=KERNEL_VMEM),
        name="attend_back",
    )(*args)


def middle_body(
    num_ref, att_ref, tok_ref, emb_ref, par_ref, cot_ref, wout_ref, w_ref,
    layer_ref, back_ref, do_ref, keep_ref, send_ref, keepo_ref, sendo_ref, vec_ref, bvec_ref,
    mid_ref, sec_ref, sect_ref, upl_ref, uplt_ref, mlp_ref, sback_ref,
):
    step = pl.program_id(0)
    tps, rows, width = att_ref.shape
    model = tok_ref.shape[1]
    wide = w_ref.shape[2] // 2
    half_wide, half_width = wide // 2, width // 2
    blocks, sub = keep_ref.shape[0], keep_ref.shape[2]
    low_core = num_ref[3] == 0

    def store(keep, send, value, half, t, at):
        for ref, is_kept in ((keep, True), (send, False)):
            chosen = jnp.where(low_core, value[:, :half], value[:, half:])
            if not is_kept:
                chosen = jnp.where(low_core, value[:, half:], value[:, :half])
            for b in range(blocks):
                ref[b, t, :, at : at + half] = chosen[b * sub : (b + 1) * sub].astype(bf16)

    @pl.when(step == 0)
    def _():
        start = tok_ref[...].astype(f32) + emb_ref[...]
        attn = None
        for t in range(tps):
            part = dot(att_ref[t], wout_ref[t][:, :width], NT)
            attn = part if attn is None else attn + part
        middle = start + attn + par_ref[2:3, :]
        mid_ref[...] = middle
        center = middle - jnp.mean(middle, axis=1, keepdims=True)
        scale = lax.rsqrt(jnp.mean(center * center, axis=1, keepdims=True) + norm_eps)
        second = (center * scale * par_ref[0:1, :] + par_ref[1:2, :]).astype(bf16)
        sec_ref[...] = second
        sect_ref[...] = second.T
        place = num_ref[0] + lax.broadcasted_iota(jnp.int32, (rows, model), 0)
        upstream = jnp.where(place < num_ref[1], cot_ref[...].astype(f32), 0.0)
        low = upstream.astype(bf16)
        upl_ref[...] = low
        uplt_ref[...] = low.T
        mlp_ref[...] = jnp.zeros_like(mlp_ref)
        sback_ref[...] = jnp.zeros_like(sback_ref)

    w_up, w_down = w_ref[0, :, :wide], w_ref[0, :, wide:]
    b_up = wout_ref[step][:, width:].astype(f32).T[0:1, :]
    hidden = dot(sec_ref[...], w_up) + b_up
    half = 0.5 * (1.0 + lax.erf(hidden * (0.5**0.5)))
    activated = (hidden * half).astype(bf16)
    mlp_ref[...] += dot(activated, w_down, NT)
    act_back = dot(upl_ref[...], w_down)
    slope = half + hidden * (jnp.exp(-0.5 * hidden * hidden) * 0.3989422804014327)
    hidden_back = (act_back * slope).astype(bf16)
    sback_ref[...] += dot(hidden_back, w_up, NT)
    bvec_ref[pl.ds(step, 1), :] = jnp.sum(hidden_back.astype(f32), axis=0, keepdims=True)
    store(keep_ref, send_ref, dot(sect_ref[...], hidden_back), half_wide, 0, 0)
    store(keep_ref, send_ref, dot(uplt_ref[...], activated), half_wide, 0, half_wide)

    @pl.when(step == pl.num_programs(0) - 1)
    def _():
        middle = mid_ref[...]
        layer_ref[...] = (middle + mlp_ref[...] + par_ref[3:4, :]).astype(bf16)
        center = middle - jnp.mean(middle, axis=1, keepdims=True)
        scale = lax.rsqrt(jnp.mean(center * center, axis=1, keepdims=True) + norm_eps)
        n = center * scale
        e = sback_ref[...]
        eg = e * par_ref[0:1, :]
        norm = scale * (
            eg
            - jnp.mean(eg, axis=1, keepdims=True)
            - n * jnp.mean(eg * n, axis=1, keepdims=True)
        )
        upstream = upl_ref[...].astype(f32)
        back = upstream + norm
        back_ref[...] = back
        low = back.astype(bf16)
        low_t = low.T
        keepo_ref[...] = jnp.zeros_like(keepo_ref)
        sendo_ref[...] = jnp.zeros_like(sendo_ref)
        for t in range(tps):
            do_ref[t] = dot(low, wout_ref[t][:, :width]).astype(bf16)
            store(keepo_ref, sendo_ref, dot(low_t, att_ref[t]), half_width, t, 0)
        vec_ref[0:1, :] = jnp.sum(e * n, axis=0, keepdims=True)
        vec_ref[1:2, :] = jnp.sum(e, axis=0, keepdims=True)
        vec_ref[2:3, :] = jnp.sum(low.astype(f32), axis=0, keepdims=True)
        vec_ref[3:4, :] = jnp.sum(upstream, axis=0, keepdims=True)
        vec_ref[4:8, :] = jnp.zeros((4, model), f32)


def middle_part(numbers, att, tokens, embedded, params, cotangent, weights, wide, blocks):
    tps, rows, width = att.shape
    model = tokens.shape[1]
    packed = weights.shape[2]
    fixed = lambda shape: pl.BlockSpec(shape, lambda i, n: (0,) * len(shape))
    mine = pl.BlockSpec((rows, model), lambda i, n: (n[2], 0))
    spare = packed - 2 * wide
    sub = model // blocks
    small = (blocks, tps, sub, 128)
    moving = pl.BlockSpec((blocks, 1, sub, wide), lambda i, n: (0, i, 0, 0))
    return pl.pallas_call(
        middle_body,
        grid_spec=pltpu.PrefetchScalarGridSpec(
            num_scalar_prefetch=1,
            grid=(tps,),
            in_specs=[
                fixed(att.shape),
                mine,
                fixed(embedded.shape),
                fixed(params.shape),
                mine,
                pl.BlockSpec((tps, model, spare), lambda i, n: (0, 0, 2 * wide // spare)),
                pl.BlockSpec((1, model, 2 * wide), lambda i, n: (i, 0, 0)),
            ],
            out_specs=[
                fixed((rows, model)),
                fixed((rows, model)),
                fixed(att.shape),
                moving,
                moving,
                fixed(small),
                fixed(small),
                fixed((8, model)),
                fixed((tps, wide)),
            ],
            scratch_shapes=[
                pltpu.VMEM((rows, model), f32),
                pltpu.VMEM((rows, model), bf16),
                pltpu.VMEM((model, rows), bf16),
                pltpu.VMEM((rows, model), bf16),
                pltpu.VMEM((model, rows), bf16),
                pltpu.VMEM((rows, model), f32),
                pltpu.VMEM((rows, model), f32),
            ],
        ),
        out_shape=[
            jax.ShapeDtypeStruct((rows, model), bf16),
            jax.ShapeDtypeStruct((rows, model), f32),
            jax.ShapeDtypeStruct(att.shape, bf16),
            jax.ShapeDtypeStruct((blocks, tps, sub, wide), bf16),
            jax.ShapeDtypeStruct((blocks, tps, sub, wide), bf16),
            jax.ShapeDtypeStruct(small, bf16),
            jax.ShapeDtypeStruct(small, bf16),
            jax.ShapeDtypeStruct((8, model), f32),
            jax.ShapeDtypeStruct((tps, wide), f32),
        ],
        cost_estimate=pl.CostEstimate(
            flops=12 * rows * model * wide * tps,
            bytes_accessed=2 * weights.size * 2,
            transcendentals=2 * rows * wide * tps,
        ),
        compiler_params=pltpu.CompilerParams(vmem_limit_bytes=KERNEL_VMEM),
        name="middle",
    )(numbers, att, tokens, embedded, params, cotangent, weights, weights)


def flip(value, axis, bit=1, size=2):
    return lax.ppermute(value, axis, [(i, i ^ bit) for i in range(size)])


def after(value, *others):
    return lax.optimization_barrier((value, *others))[0]


def swap_rows(value):
    return lax.all_to_all(value, "tp", 0, 0, tiled=True)


def gather_dp(value, dps, axis):
    if dps != 2:
        return lax.all_gather(value, "dp", axis=axis, tiled=True)
    return pair(value, "dp", axis)


def pair(value, axis_name, axis):
    other = flip(value, axis_name)
    first = lax.axis_index(axis_name) == 0
    return jnp.concatenate(
        (jnp.where(first, value, other), jnp.where(first, other, value)), axis=axis
    )


def add_low(*terms):
    total = terms[0].astype(f32)
    for term in terms[1:]:
        total = total + term.astype(f32)
    return total.astype(bf16)


def sum_vectors(value, dps, tps):
    for axis in ("core", "y"):
        value = value + flip(value, axis)
    if dps == 2:
        value = value + flip(value, "dp")
    else:
        value = lax.psum(value, "dp")
    for bit in (1, 2):
        value = value + flip(value, "tp", bit, tps)
    return value


def reduce_projections(grad, dps):
    if dps != 2:
        grad = lax.psum_scatter(grad, ("dp", "y", "core"), scatter_dimension=0, tiled=True)
        return lax.all_gather(grad, ("y", "core"), axis=0, tiled=True)
    dp, y, core = lax.axis_index("dp"), lax.axis_index("y"), lax.axis_index("core")
    size = grad.shape[0] // 8
    grad = grad.reshape(2, 2, 2 * size, -1)
    pick = lambda v, i, axis: lax.dynamic_index_in_dim(v, i, axis, False)
    grad = add_low(pick(grad, core, 1), flip(pick(grad, 1 - core, 1), "core"))
    grad = add_low(pick(grad, dp, 0), flip(pick(grad, 1 - dp, 0), "dp"))
    grad = grad.reshape(2, size, -1)
    grad = add_low(pick(grad, y, 0), flip(pick(grad, 1 - y, 0), "y"))
    return pair(pair(grad, "y", 0), "core", 0)


def unpack_body(half, half_out, core_ref, mine_ref, other_ref, up_ref, down_ref, out_ref):
    low_core = core_ref[0] == 0
    mine, other = mine_ref[...].astype(f32), other_ref[...].astype(f32)
    halves = (jnp.where(low_core, mine, other), jnp.where(low_core, other, mine))
    for i, value in enumerate(halves):
        up_ref[:, i * half : (i + 1) * half] = value[:, :half]
        down_ref[i * half : (i + 1) * half, :] = value[:, half : 2 * half].T
        turned = value[:, 2 * half :].T
        out_ref[i * half_out : (i + 1) * half_out, :] = turned[:half_out]


def unpack(mine, core, half, half_out):
    other = flip(mine, "core")
    part = mine.shape[0]
    shapes = ((part, 2 * half), (2 * half, part), (2 * half_out, part))
    if part % 128:
        first = core == 0
        halves = (jnp.where(first, mine, other), jnp.where(first, other, mine))
        pick = lambda a, b: jnp.concatenate([h[:, a:b] for h in halves], axis=1).astype(f32)
        return (
            pick(0, half),
            pick(half, 2 * half).T,
            pick(2 * half, 2 * half + half_out).T,
        )
    fixed = lambda shape: pl.BlockSpec(shape, lambda i, n: (0,) * len(shape))
    return pl.pallas_call(
        functools.partial(unpack_body, half, half_out),
        grid_spec=pltpu.PrefetchScalarGridSpec(
            num_scalar_prefetch=1,
            grid=(1,),
            in_specs=[fixed(mine.shape)] * 2,
            out_specs=[fixed(shape) for shape in shapes],
        ),
        out_shape=[jax.ShapeDtypeStruct(shape, f32) for shape in shapes],
        name="unpack",
    )(core[None].astype(jnp.int32), mine, other)


def spread_rows(value, tps):
    copies = swap_rows(jnp.broadcast_to(value[None], (tps, *value.shape)))
    return copies.reshape(tps * value.shape[0], value.shape[1])


def on_device(
    dps, tps,
    tokens, time_steps, lengths, time_table, norm_gains, norm_biases, w_qkv, b_qv, w_out,
    out_biases, w_up, b_up, w_down, cotangent,
):
    _, row_count, model = tokens.shape
    local = b_qv.shape[1]
    wide = b_up.shape[0]
    part = w_up.shape[0]
    steps_in_table = time_table.shape[0]
    rows = row_count // tps
    dp, tp = lax.axis_index("dp"), lax.axis_index("tp")
    core = lax.axis_index("core")
    ctx = 2 * lax.axis_index("y") + core

    all_steps = gather_dp(time_steps, dps, 0)
    small = jnp.concatenate((norm_gains, norm_biases, out_biases, time_table[all_steps]))
    small = gather_dp(small, dps, 1).astype(f32)
    embedded = lax.dynamic_slice_in_dim(small, 6 + dp, 1, 0)
    gain_first, shift_first = small[0:1], small[2:3]
    params = jnp.stack(
        (small[1], small[3], small[4], small[5], small[1], small[1], small[1], small[1])
    )

    qkv_mine = jnp.concatenate((w_qkv[0], w_qkv[1], w_qkv[2]), axis=1)
    qkv_full = gather_dp(qkv_mine, dps, 0)
    slab = part // 4
    spare = -(-(local + 1) // 128) * 128
    piece = jnp.concatenate(
        (
            lax.dynamic_slice_in_dim(w_up, ctx * slab, slab, 0),
            lax.dynamic_slice_in_dim(w_down, ctx * slab, slab, 1).T,
            lax.dynamic_slice_in_dim(w_out, ctx * slab, slab, 1).T,
            lax.dynamic_slice_in_dim(b_up, dp * part + ctx * slab, slab, 0)[:, None],
            jnp.zeros((slab, spare - local - 1), bf16),
        ),
        axis=1,
    )
    weights = lax.all_gather(piece, ("tp", "dp", "y", "core"), axis=0, tiled=True)
    weights = weights.reshape(tps, model, 2 * wide + spare)

    flat = tokens.reshape(row_count, model)
    start = flat.astype(f32) + embedded
    center = start - jnp.mean(start, axis=1, keepdims=True)
    scale = lax.rsqrt(jnp.mean(center * center, axis=1, keepdims=True) + norm_eps)
    normed = (center * scale * gain_first + shift_first).astype(bf16)
    bias = b_qv.astype(f32)
    kv_bias = jnp.concatenate((jnp.zeros((local,), f32), bias[1]))[:, None]
    kv = lax.dot_general(
        qkv_full[:, local:], normed, (((0,), (1,)), ((), ())), preferred_element_type=f32
    )
    kv = (kv + kv_bias).astype(bf16)
    queries = (dot(normed, qkv_full[:, :local]) + bias[0]).astype(bf16) * bf16(HEAD**-0.5)

    place = jnp.arange(row_count)[None, :]

    def key_bias(owner):
        return jnp.where(owner * row_count + place < lengths[0], 0.0, -1e30).astype(f32)

    biases = [key_bias(ctx ^ b) for b in range(4)]
    kv_1 = flip(kv, "core")
    kv_2 = flip(kv, "y")
    carry = attend(queries, (kv, kv_1), biases[:2], None, False)
    kv_2 = after(kv_2, *carry)
    kv_3 = flip(kv_2, "core")
    attended, log_total, attended_low = attend(queries, (kv_2, kv_3), biases[2:], carry, True)

    swapped = swap_rows(attended_low.reshape(tps, rows, local))
    numbers = jnp.stack((ctx * row_count + tp * rows, lengths[0], tp, core)).astype(jnp.int32)
    layer_rows, middle_back, output_back, keep, send, keep_o, send_o, vectors, grad_b_up = middle_part(
        numbers,
        swapped,
        flat,
        embedded,
        params,
        cotangent.reshape(row_count, model),
        weights,
        wide,
        2 * dps,
    )
    output_back = swap_rows(output_back).reshape(row_count, local)

    grad_packed = jnp.concatenate(
        (add_low(keep, flip(send, "core")), add_low(keep_o, flip(send_o, "core"))), axis=-1
    )
    grad_packed = grad_packed.reshape(2 * dps * tps * part // 2, -1)
    grad_packed = lax.psum_scatter(grad_packed, ("dp", "y"), scatter_dimension=0, tiled=True)
    grad_packed = lax.psum_scatter(grad_packed, "tp", scatter_dimension=0, tiled=True)

    layer_out = spread_rows(after(layer_rows, output_back), tps)
    dq, dkv_2, dkv_3 = attend_back(
        queries, output_back, attended, log_total, (kv_2, kv_3), biases[2:], None
    )
    far = add_low(dkv_2, flip(dkv_3, "core"))
    dq = after(dq, far)
    far = flip(far, "y")
    dq, dkv_0, dkv_1 = attend_back(
        queries, output_back, attended, log_total, (kv, kv_1), biases[:2], dq
    )
    dkv_1, layer_out = lax.optimization_barrier((dkv_1, layer_out))
    near = flip(dkv_1, "core")
    dkv = add_low(dkv_0, near, far)

    back = dot(dq, qkv_full[:, :local], NT) + lax.dot_general(
        dkv, qkv_full[:, local:], (((0,), (1,)), ((), ())), preferred_element_type=f32
    )
    back = swap_rows(back.astype(bf16).reshape(tps, rows, model))
    grad_qkv = jnp.concatenate(
        (
            lax.dot_general(normed, dq, (((0,), (0,)), ((), ())), preferred_element_type=f32),
            lax.dot_general(normed, dkv, (((0,), (1,)), ((), ())), preferred_element_type=f32),
        ),
        axis=1,
    ).astype(bf16)
    grad_qkv = reduce_projections(grad_qkv, dps).astype(f32)
    grad_w_qkv = jnp.stack([grad_qkv[:, i * local : (i + 1) * local] for i in range(3)])

    e = jnp.sum(back.astype(f32), axis=0)
    mine = lax.dynamic_slice_in_dim(flat, tp * rows, rows, 0).astype(f32) + embedded
    center = mine - jnp.mean(mine, axis=1, keepdims=True)
    scale = lax.rsqrt(jnp.mean(center * center, axis=1, keepdims=True) + norm_eps)
    n = center * scale
    eg = e * gain_first
    start_norm = scale * (
        eg - jnp.mean(eg, axis=1, keepdims=True) - n * jnp.mean(eg * n, axis=1, keepdims=True)
    )
    grad_rows = middle_back + start_norm
    grad_tokens = spread_rows(grad_rows.astype(bf16), tps).astype(f32)

    token_sums = jnp.zeros((dps, model), f32)
    token_sums = lax.dynamic_update_slice_in_dim(
        token_sums, jnp.sum(grad_rows, axis=0, keepdims=True), dp, 0
    )
    qv_sums = jnp.concatenate(
        (jnp.sum(dq.astype(f32), axis=0), jnp.sum(dkv[local:].astype(f32), axis=1))
    )
    qv_slots = jnp.zeros((tps, 2 * local), f32)
    qv_slots = lax.dynamic_update_slice_in_dim(qv_slots, qv_sums[None], tp, 0)
    sums = jnp.concatenate(
        (
            vectors[:4],
            jnp.sum(e * n, axis=0, keepdims=True),
            jnp.sum(e, axis=0, keepdims=True),
            token_sums,
            grad_b_up.reshape(-1, model),
            qv_slots.reshape(-1, model),
        )
    )
    grad_w_up, grad_w_down, grad_w_out = unpack(
        pair(grad_packed, "y", 0), core, wide // 2, local // 2
    )
    sums = sum_vectors(sums, dps, tps)
    own = lax.dynamic_slice_in_dim(sums, dp * part, part, 1)
    grad_gains = jnp.stack((own[4], own[0]))
    grad_shifts = jnp.stack((own[5], own[1]))
    grad_out_biases = jnp.stack((own[2], own[3]))
    at = 6 + dps
    b_rows = grad_b_up.size // model
    grad_b_up = lax.dynamic_slice_in_dim(
        sums[at : at + b_rows].reshape(-1), tp * wide, wide, 0
    )
    grad_b_qv = lax.dynamic_index_in_dim(
        sums[at + b_rows :].reshape(tps, 2, local), tp, 0, False
    )
    step_rows = jnp.arange(steps_in_table)[:, None]
    grad_table = jnp.zeros((steps_in_table, part), f32)
    for s in range(dps):
        grad_table = grad_table + jnp.where(step_rows == all_steps[s], own[6 + s][None], 0.0)
    return (
        layer_out[None],
        grad_tokens[None],
        grad_table,
        grad_gains,
        grad_shifts,
        grad_w_qkv,
        grad_b_qv,
        grad_w_out,
        grad_out_biases,
        grad_w_up,
        grad_b_up,
        grad_w_down,
    )


def solution(mesh):
    in_specs = (
        P("dp", ("y", "core"), None),
        P("dp"),
        P("dp"),
        P(None, "dp"),
        P(None, "dp"),
        P(None, "dp"),
        P(None, "dp", "tp"),
        P(None, "tp"),
        P("tp", "dp"),
        P(None, "dp"),
        P("dp", "tp"),
        P("tp"),
        P("tp", "dp"),
        P("dp", ("y", "core"), None),
    )
    out_specs = (
        P("dp", ("y", "core"), None),
        P("dp", ("y", "core"), None),
        P(None, "dp"),
        P(None, "dp"),
        P(None, "dp"),
        P(None, "dp", "tp"),
        P(None, "tp"),
        P("tp", "dp"),
        P(None, "dp"),
        P("dp", "tp"),
        P("tp"),
        P("tp", "dp"),
    )
    sizes = (mesh.shape["dp"], mesh.shape["tp"])
    fine = jax.sharding.Mesh(
        mesh.devices.reshape(sizes[0], 2, mesh.shape["ctx"] // 2, sizes[1]),
        ("dp", "y", "core", "tp"),
    )
    return jax.shard_map(
        functools.partial(on_device, *sizes),
        mesh=fine,
        in_specs=in_specs,
        out_specs=out_specs,
        check_vma=False,
    )
```

```python
import functools

import jax
import jax.numpy as jnp
from jax import lax
from jax.experimental import pallas as pl
from jax.experimental.pallas import tpu as pltpu
from jax.sharding import PartitionSpec as P

HEAD = 64
norm_eps = 1e-05
NT = (((1,), (1,)), ((), ()))
NN = (((1,), (0,)), ((), ()))
f32 = jnp.float32
bf16 = jnp.bfloat16
KERNEL_VMEM = 60 * 2**20


def dot(a, b, dims=NN):
    return lax.dot_general(a, b, dims, preferred_element_type=f32)


def attend_body(heads, piece, blocks, first, last, q_ref, *refs):
    kv_refs, bias_refs, refs = refs[:blocks], refs[blocks : 2 * blocks], refs[2 * blocks :]
    if not first:
        (part_ref, old_ref), refs = refs[:2], refs[2:]
    out_ref, stat_ref, score_ref = refs[0], refs[1], refs[-1]
    rows = q_ref.shape[0]
    length = kv_refs[0].shape[1]
    width = heads * HEAD
    pieces = [(b, c) for b in range(blocks) for c in range(0, length, piece)]
    stats = []
    for h in range(heads):
        cols = slice(h * HEAD, (h + 1) * HEAD)
        vals = slice(width + h * HEAD, width + (h + 1) * HEAD)
        q = q_ref[:, cols]
        peak = None
        for b, c in pieces:
            scores = dot(q, kv_refs[b][cols, c : c + piece]) + bias_refs[b][:, c : c + piece]
            score_ref[h, :, b * length + c : b * length + c + piece] = scores
            for j in range(0, piece, 128):
                part = scores[:, j : j + 128]
                peak = part if peak is None else jnp.maximum(peak, part)
        peak = jnp.max(peak, axis=1, keepdims=True)
        if not first:
            old_peak = old_ref[:, h : h + 1]
            peak = jnp.maximum(peak, old_peak)
        total, summed = None, None
        for b, c in pieces:
            weights = jnp.exp(score_ref[h, :, b * length + c : b * length + c + piece] - peak)
            for j in range(0, piece, 128):
                part = weights[:, j : j + 128]
                total = part if total is None else total + part
            part = dot(weights.astype(bf16), kv_refs[b][vals, c : c + piece], NT)
            summed = part if summed is None else summed + part
        total = jnp.sum(total, axis=1, keepdims=True)
        if not first:
            shrink = jnp.exp(old_peak - peak)
            total = total + old_ref[:, 8 + h : 9 + h] * shrink
            summed = summed + part_ref[:, cols] * shrink
        if last:
            summed = summed / total
        stats.append((peak, total))
        out_ref[:, cols] = summed
        if last:
            refs[2][:, cols] = summed.astype(bf16)
    lane = lax.broadcasted_iota(jnp.int32, (rows, 128), 1)
    packed = jnp.zeros((rows, 128), f32)
    for h, (peak, total) in enumerate(stats):
        if last:
            packed = jnp.where(lane == h, peak + jnp.log(total), packed)
        else:
            packed = jnp.where(lane == h, peak, packed)
            packed = jnp.where(lane == 8 + h, total, packed)
    stat_ref[...] = packed


def row_spec(rows, width):
    return pl.BlockSpec((rows, width), lambda i: (i, 0))


def whole_spec(array):
    zeros = (0,) * array.ndim
    return pl.BlockSpec(array.shape, lambda i: zeros)


def attend(queries, kvs, biases, carry, last, rows=128, piece=512):
    count, width = queries.shape
    length = kvs[0].shape[1]
    heads = width // HEAD
    keys = length * len(kvs)
    args = [queries, *kvs, *biases]
    specs = [row_spec(rows, width)] + [whole_spec(a) for a in args[1:]]
    if carry is not None:
        args += list(carry)
        specs += [row_spec(rows, width), row_spec(rows, 128)]
    return pl.pallas_call(
        functools.partial(attend_body, heads, piece, len(kvs), carry is None, last),
        grid=(count // rows,),
        in_specs=specs,
        out_specs=[row_spec(rows, width), row_spec(rows, 128)]
        + [row_spec(rows, width)] * last,
        out_shape=[
            jax.ShapeDtypeStruct((count, width), f32),
            jax.ShapeDtypeStruct((count, 128), f32),
        ]
        + [jax.ShapeDtypeStruct((count, width), bf16)] * last,
        scratch_shapes=[pltpu.VMEM((heads, rows, keys), f32)],
        cost_estimate=pl.CostEstimate(
            flops=16 * count * keys * width,
            bytes_accessed=count * width * 6 + keys * width * 4,
            transcendentals=count * keys * heads,
        ),
        compiler_params=pltpu.CompilerParams(vmem_limit_bytes=KERNEL_VMEM),
        name="attend",
    )(*args)


def attend_back_body(heads, piece, blocks, first, q_ref, do_ref, att_ref, log_ref, *refs):
    kv_refs, bias_refs, refs = refs[:blocks], refs[blocks : 2 * blocks], refs[2 * blocks :]
    if not first:
        part_ref, refs = refs[0], refs[1:]
    dq_ref, dkv_refs, sum_refs = refs[0], refs[1 : 1 + blocks], refs[1 + blocks :]
    step = pl.program_id(0)
    length = kv_refs[0].shape[1]
    width = heads * HEAD

    @pl.when(step == 0)
    def _():
        for sum_ref in sum_refs:
            sum_ref[...] = jnp.zeros_like(sum_ref)

    q, do = q_ref[...], do_ref[...]
    q_t, do_t = q.T, do.T
    product = do.astype(f32) * att_ref[...]
    for h in range(heads):
        cols = slice(h * HEAD, (h + 1) * HEAD)
        vals = slice(width + h * HEAD, width + (h + 1) * HEAD)
        delta = jnp.sum(product[:, cols], axis=1, keepdims=True)
        log_total = log_ref[:, h : h + 1]
        dq = None
        for b in range(blocks):
            for c in range(0, length, piece):
                span = slice(c, c + piece)
                scores = dot(q[:, cols], kv_refs[b][cols, span]) + bias_refs[b][:, span]
                probs = jnp.exp(scores - log_total)
                grads = dot(do[:, cols], kv_refs[b][vals, span])
                score_grad = (probs * (grads - delta)).astype(bf16)
                part = dot(score_grad, kv_refs[b][cols, span], NT)
                dq = part if dq is None else dq + part
                sum_refs[b][cols, span] += dot(q_t[cols, :], score_grad)
                sum_refs[b][vals, span] += dot(do_t[cols, :], probs.astype(bf16))
        dq = dq * HEAD ** (-0.5)
        if not first:
            dq = dq + part_ref[:, cols]
        dq_ref[:, cols] = dq.astype(dq_ref.dtype)

    @pl.when(step == pl.num_programs(0) - 1)
    def _():
        for dkv_ref, sum_ref in zip(dkv_refs, sum_refs):
            dkv_ref[...] = sum_ref[...].astype(dkv_ref.dtype)


def attend_back(queries, do, att, log_total, kvs, biases, part, rows=256, piece=1024):
    count, width = queries.shape
    length = kvs[0].shape[1]
    heads = width // HEAD
    keys = length * len(kvs)
    args = [queries, do, att, log_total, *kvs, *biases]
    specs = [row_spec(rows, width)] * 3 + [row_spec(rows, 128)]
    specs += [whole_spec(a) for a in args[4:]]
    if part is not None:
        args.append(part)
        specs.append(row_spec(rows, width))
    return pl.pallas_call(
        functools.partial(attend_back_body, heads, piece, len(kvs), part is None),
        grid=(count // rows,),
        in_specs=specs,
        out_specs=[row_spec(rows, width)] + [whole_spec(kv) for kv in kvs],
        out_shape=[jax.ShapeDtypeStruct((count, width), f32 if part is None else bf16)]
        + [jax.ShapeDtypeStruct(kv.shape, bf16) for kv in kvs],
        scratch_shapes=[pltpu.VMEM(kv.shape, f32) for kv in kvs],
        cost_estimate=pl.CostEstimate(
            flops=4 * count * keys * width,
            bytes_accessed=count * width * 12 + keys * width * 8,
            transcendentals=count * keys * heads,
        ),
        compiler_params=pltpu.CompilerParams(vmem_limit_bytes=KERNEL_VMEM),
        name="attend_back",
    )(*args)


def middle_body(
    num_ref, att_ref, tok_ref, emb_ref, par_ref, cot_ref, wout_ref, w_ref,
    layer_ref, back_ref, do_ref, keep_ref, send_ref, keepo_ref, sendo_ref, vec_ref, bvec_ref,
    mid_ref, sec_ref, sect_ref, upl_ref, uplt_ref, mlp_ref, sback_ref,
):
    step = pl.program_id(0)
    tps, rows, width = att_ref.shape
    model = tok_ref.shape[1]
    wide = w_ref.shape[2] // 2
    blocks, sub = keep_ref.shape[0], keep_ref.shape[2]
    low_core = num_ref[3] == 0

    def store(keep, send, left, right, t, at):
        half = right.shape[1] // 2
        low, high = right[:, :half], right[:, half:]
        for ref, chosen in (
            (keep, jnp.where(low_core, low, high)),
            (send, jnp.where(low_core, high, low)),
        ):
            value = dot(left, chosen)
            for b in range(blocks):
                ref[b, t, :, at : at + half] = value[b * sub : (b + 1) * sub].astype(bf16)

    @pl.when(step == 0)
    def _():
        start = tok_ref[...].astype(f32) + emb_ref[...]
        attn = None
        for t in range(tps):
            part = dot(att_ref[t], wout_ref[t][:, :width], NT)
            attn = part if attn is None else attn + part
        middle = start + attn + par_ref[2:3, :]
        mid_ref[...] = middle
        center = middle - jnp.mean(middle, axis=1, keepdims=True)
        scale = lax.rsqrt(jnp.mean(center * center, axis=1, keepdims=True) + norm_eps)
        second = (center * scale * par_ref[0:1, :] + par_ref[1:2, :]).astype(bf16)
        sec_ref[...] = second
        sect_ref[...] = second.T
        place = num_ref[0] + lax.broadcasted_iota(jnp.int32, (rows, model), 0)
        upstream = jnp.where(place < num_ref[1], cot_ref[...].astype(f32), 0.0)
        low = upstream.astype(bf16)
        upl_ref[...] = low
        uplt_ref[...] = low.T
        mlp_ref[...] = jnp.zeros_like(mlp_ref)
        sback_ref[...] = jnp.zeros_like(sback_ref)

    w_up, w_down = w_ref[0, :, :wide], w_ref[0, :, wide:]
    b_up = wout_ref[step][:, width:].astype(f32).T[0:1, :]
    hidden = dot(sec_ref[...], w_up) + b_up
    half = 0.5 * (1.0 + lax.erf(hidden * (0.5**0.5)))
    activated = (hidden * half).astype(bf16)
    mlp_ref[...] += dot(activated, w_down, NT)
    act_back = dot(upl_ref[...], w_down)
    slope = half + hidden * (jnp.exp(-0.5 * hidden * hidden) * 0.3989422804014327)
    hidden_back = (act_back * slope).astype(bf16)
    sback_ref[...] += dot(hidden_back, w_up, NT)
    bvec_ref[pl.ds(step, 1), :] = jnp.sum(hidden_back.astype(f32), axis=0, keepdims=True)
    store(keep_ref, send_ref, sect_ref[...], hidden_back, 0, 0)
    store(keep_ref, send_ref, uplt_ref[...], activated, 0, wide // 2)

    @pl.when(step == pl.num_programs(0) - 1)
    def _():
        middle = mid_ref[...]
        layer_ref[...] = (middle + mlp_ref[...] + par_ref[3:4, :]).astype(bf16)
        center = middle - jnp.mean(middle, axis=1, keepdims=True)
        scale = lax.rsqrt(jnp.mean(center * center, axis=1, keepdims=True) + norm_eps)
        n = center * scale
        e = sback_ref[...]
        eg = e * par_ref[0:1, :]
        norm = scale * (
            eg
            - jnp.mean(eg, axis=1, keepdims=True)
            - n * jnp.mean(eg * n, axis=1, keepdims=True)
        )
        upstream = upl_ref[...].astype(f32)
        back = upstream + norm
        back_ref[...] = back
        low = back.astype(bf16)
        low_t = low.T
        keepo_ref[...] = jnp.zeros_like(keepo_ref)
        sendo_ref[...] = jnp.zeros_like(sendo_ref)
        for t in range(tps):
            do_ref[t] = dot(low, wout_ref[t][:, :width]).astype(bf16)
            store(keepo_ref, sendo_ref, low_t, att_ref[t], t, 0)
        vec_ref[0:1, :] = jnp.sum(e * n, axis=0, keepdims=True)
        vec_ref[1:2, :] = jnp.sum(e, axis=0, keepdims=True)
        vec_ref[2:3, :] = jnp.sum(low.astype(f32), axis=0, keepdims=True)
        vec_ref[3:4, :] = jnp.sum(upstream, axis=0, keepdims=True)
        vec_ref[4:8, :] = jnp.zeros((4, model), f32)


def middle_part(numbers, att, tokens, embedded, params, cotangent, weights, wide, blocks):
    tps, rows, width = att.shape
    model = tokens.shape[1]
    packed = weights.shape[2]
    fixed = lambda shape: pl.BlockSpec(shape, lambda i, n: (0,) * len(shape))
    mine = pl.BlockSpec((rows, model), lambda i, n: (n[2], 0))
    spare = packed - 2 * wide
    sub = model // blocks
    small = (blocks, tps, sub, 128)
    moving = pl.BlockSpec((blocks, 1, sub, wide), lambda i, n: (0, i, 0, 0))
    return pl.pallas_call(
        middle_body,
        grid_spec=pltpu.PrefetchScalarGridSpec(
            num_scalar_prefetch=1,
            grid=(tps,),
            in_specs=[
                fixed(att.shape),
                mine,
                fixed(embedded.shape),
                fixed(params.shape),
                mine,
                pl.BlockSpec((tps, model, spare), lambda i, n: (0, 0, 2 * wide // spare)),
                pl.BlockSpec((1, model, 2 * wide), lambda i, n: (i, 0, 0)),
            ],
            out_specs=[
                fixed((rows, model)),
                fixed((rows, model)),
                fixed(att.shape),
                moving,
                moving,
                fixed(small),
                fixed(small),
                fixed((8, model)),
                fixed((tps, wide)),
            ],
            scratch_shapes=[
                pltpu.VMEM((rows, model), f32),
                pltpu.VMEM((rows, model), bf16),
                pltpu.VMEM((model, rows), bf16),
                pltpu.VMEM((rows, model), bf16),
                pltpu.VMEM((model, rows), bf16),
                pltpu.VMEM((rows, model), f32),
                pltpu.VMEM((rows, model), f32),
            ],
        ),
        out_shape=[
            jax.ShapeDtypeStruct((rows, model), bf16),
            jax.ShapeDtypeStruct((rows, model), f32),
            jax.ShapeDtypeStruct(att.shape, bf16),
            jax.ShapeDtypeStruct((blocks, tps, sub, wide), bf16),
            jax.ShapeDtypeStruct((blocks, tps, sub, wide), bf16),
            jax.ShapeDtypeStruct(small, bf16),
            jax.ShapeDtypeStruct(small, bf16),
            jax.ShapeDtypeStruct((8, model), f32),
            jax.ShapeDtypeStruct((tps, wide), f32),
        ],
        cost_estimate=pl.CostEstimate(
            flops=12 * rows * model * wide * tps,
            bytes_accessed=2 * weights.size * 2,
            transcendentals=2 * rows * wide * tps,
        ),
        compiler_params=pltpu.CompilerParams(vmem_limit_bytes=KERNEL_VMEM),
        name="middle",
    )(numbers, att, tokens, embedded, params, cotangent, weights, weights)


def flip(value, axis, bit=1, size=2):
    return lax.ppermute(value, axis, [(i, i ^ bit) for i in range(size)])


def after(value, *others):
    return lax.optimization_barrier((value, *others))[0]


def swap_rows(value):
    return lax.all_to_all(value, "tp", 0, 0, tiled=True)


def gather_dp(value, dps, axis):
    if dps != 2:
        return lax.all_gather(value, "dp", axis=axis, tiled=True)
    return pair(value, "dp", axis)


def pair(value, axis_name, axis):
    other = flip(value, axis_name)
    first = lax.axis_index(axis_name) == 0
    return jnp.concatenate(
        (jnp.where(first, value, other), jnp.where(first, other, value)), axis=axis
    )


def add_low(*terms):
    total = terms[0].astype(f32)
    for term in terms[1:]:
        total = total + term.astype(f32)
    return total.astype(bf16)


def sum_vectors(value, dps, tps, then):
    for axis in ("core", "y"):
        value = value + flip(value, axis)
    value = after(value, then)
    if dps == 2:
        value = value + flip(value, "dp")
    else:
        value = lax.psum(value, "dp")
    for bit in (1, 2):
        value = value + flip(value, "tp", bit, tps)
    return value


def reduce_projections(grad, dps):
    if dps != 2:
        grad = lax.psum_scatter(grad, ("dp", "y", "core"), scatter_dimension=0, tiled=True)
        return lax.all_gather(grad, ("y", "core"), axis=0, tiled=True)
    dp, y, core = lax.axis_index("dp"), lax.axis_index("y"), lax.axis_index("core")
    size = grad.shape[0] // 8
    grad = grad.reshape(2, 2, 2 * size, -1)
    pick = lambda v, i, axis: lax.dynamic_index_in_dim(v, i, axis, False)
    grad = add_low(pick(grad, core, 1), flip(pick(grad, 1 - core, 1), "core"))
    grad = add_low(pick(grad, dp, 0), flip(pick(grad, 1 - dp, 0), "dp"))
    grad = grad.reshape(2, size, -1)
    grad = add_low(pick(grad, y, 0), flip(pick(grad, 1 - y, 0), "y"))
    return pair(pair(grad, "y", 0), "core", 0)


def join_body(keep_ref, send_ref, keepo_ref, sendo_ref, out_ref):
    wide = keep_ref.shape[-1]
    for t in range(keep_ref.shape[1]):
        total = keep_ref[0, t].astype(f32) + send_ref[0, t].astype(f32)
        out_ref[0, t, :, :wide] = total.astype(bf16)
        total = keepo_ref[0, t].astype(f32) + sendo_ref[0, t].astype(f32)
        out_ref[0, t, :, wide:] = total.astype(bf16)


def join(keep, send, keep_o, send_o):
    blocks, tps, sub, wide = keep.shape
    spec = lambda last: pl.BlockSpec((1, tps, sub, last), lambda i: (i, 0, 0, 0))
    return pl.pallas_call(
        join_body,
        grid=(blocks,),
        in_specs=[spec(wide), spec(wide), spec(128), spec(128)],
        out_specs=spec(wide + 128),
        out_shape=jax.ShapeDtypeStruct((blocks, tps, sub, wide + 128), bf16),
        cost_estimate=pl.CostEstimate(
            flops=keep.size, bytes_accessed=7 * keep.size, transcendentals=0
        ),
        name="join",
    )(keep, send, keep_o, send_o)


def unpack_body(half, half_out, core_ref, mine_ref, other_ref, up_ref, down_ref, out_ref):
    low_core = core_ref[0] == 0
    mine, other = mine_ref[...].astype(f32), other_ref[...].astype(f32)
    halves = (jnp.where(low_core, mine, other), jnp.where(low_core, other, mine))
    for i, value in enumerate(halves):
        up_ref[:, i * half : (i + 1) * half] = value[:, :half]
        down_ref[i * half : (i + 1) * half, :] = value[:, half : 2 * half].T
        turned = value[:, 2 * half :].T
        out_ref[i * half_out : (i + 1) * half_out, :] = turned[:half_out]


def unpack(mine, other, core, half, half_out):
    part = mine.shape[0]
    shapes = ((part, 2 * half), (2 * half, part), (2 * half_out, part))
    if part % 128:
        first = core == 0
        halves = (jnp.where(first, mine, other), jnp.where(first, other, mine))
        pick = lambda a, b: jnp.concatenate([h[:, a:b] for h in halves], axis=1).astype(f32)
        return (
            pick(0, half),
            pick(half, 2 * half).T,
            pick(2 * half, 2 * half + half_out).T,
        )
    fixed = lambda shape: pl.BlockSpec(shape, lambda i, n: (0,) * len(shape))
    return pl.pallas_call(
        functools.partial(unpack_body, half, half_out),
        grid_spec=pltpu.PrefetchScalarGridSpec(
            num_scalar_prefetch=1,
            grid=(1,),
            in_specs=[fixed(mine.shape)] * 2,
            out_specs=[fixed(shape) for shape in shapes],
        ),
        out_shape=[jax.ShapeDtypeStruct(shape, f32) for shape in shapes],
        name="unpack",
    )(core[None].astype(jnp.int32), mine, other)


def spread_rows(value, tps):
    copies = swap_rows(jnp.broadcast_to(value[None], (tps, *value.shape)))
    return copies.reshape(tps * value.shape[0], value.shape[1])


def on_device(
    dps, tps,
    tokens, time_steps, lengths, time_table, norm_gains, norm_biases, w_qkv, b_qv, w_out,
    out_biases, w_up, b_up, w_down, cotangent,
):
    _, row_count, model = tokens.shape
    local = b_qv.shape[1]
    wide = b_up.shape[0]
    part = w_up.shape[0]
    steps_in_table = time_table.shape[0]
    rows = row_count // tps
    dp, tp = lax.axis_index("dp"), lax.axis_index("tp")
    core = lax.axis_index("core")
    ctx = 2 * lax.axis_index("y") + core

    all_steps = gather_dp(time_steps, dps, 0)
    small = jnp.concatenate((norm_gains, norm_biases, out_biases, time_table[all_steps]))
    small = gather_dp(small, dps, 1).astype(f32)
    embedded = lax.dynamic_slice_in_dim(small, 6 + dp, 1, 0)
    gain_first, shift_first = small[0:1], small[2:3]
    params = jnp.stack(
        (small[1], small[3], small[4], small[5], small[1], small[1], small[1], small[1])
    )

    qkv_mine = jnp.concatenate((w_qkv[0], w_qkv[1], w_qkv[2]), axis=1)
    qkv_full = gather_dp(qkv_mine, dps, 0)
    slab = part // 4
    spare = -(-(local + 1) // 128) * 128
    piece = jnp.concatenate(
        (
            lax.dynamic_slice_in_dim(w_up, ctx * slab, slab, 0),
            lax.dynamic_slice_in_dim(w_down, ctx * slab, slab, 1).T,
            lax.dynamic_slice_in_dim(w_out, ctx * slab, slab, 1).T,
            lax.dynamic_slice_in_dim(b_up, dp * part + ctx * slab, slab, 0)[:, None],
            jnp.zeros((slab, spare - local - 1), bf16),
        ),
        axis=1,
    )
    weights = lax.all_gather(piece, ("tp", "dp", "y", "core"), axis=0, tiled=True)
    weights = weights.reshape(tps, model, 2 * wide + spare)

    flat = tokens.reshape(row_count, model)
    start = flat.astype(f32) + embedded
    center = start - jnp.mean(start, axis=1, keepdims=True)
    scale = lax.rsqrt(jnp.mean(center * center, axis=1, keepdims=True) + norm_eps)
    normed = (center * scale * gain_first + shift_first).astype(bf16)
    bias = b_qv.astype(f32)
    kv_bias = jnp.concatenate((jnp.zeros((local,), f32), bias[1]))[:, None]
    kv = lax.dot_general(
        qkv_full[:, local:], normed, (((0,), (1,)), ((), ())), preferred_element_type=f32
    )
    kv = (kv + kv_bias).astype(bf16)
    queries = (dot(normed, qkv_full[:, :local]) + bias[0]).astype(bf16) * bf16(HEAD**-0.5)

    place = jnp.arange(row_count)[None, :]

    def key_bias(owner):
        return jnp.where(owner * row_count + place < lengths[0], 0.0, -1e30).astype(f32)

    biases = [key_bias(ctx ^ b) for b in range(4)]
    kv_1 = flip(kv, "core")
    kv_2 = flip(kv, "y")
    carry = attend(queries, (kv, kv_1), biases[:2], None, False)
    kv_2 = after(kv_2, *carry)
    kv_3 = flip(kv_2, "core")
    attended, log_total, attended_low = attend(queries, (kv_2, kv_3), biases[2:], carry, True)

    swapped = swap_rows(attended_low.reshape(tps, rows, local))
    numbers = jnp.stack((ctx * row_count + tp * rows, lengths[0], tp, core)).astype(jnp.int32)
    layer_rows, middle_back, output_back, keep, send, keep_o, send_o, vectors, grad_b_up = middle_part(
        numbers,
        swapped,
        flat,
        embedded,
        params,
        cotangent.reshape(row_count, model),
        weights,
        wide,
        2 * dps,
    )
    output_back = swap_rows(output_back).reshape(row_count, local)

    send, send_o, output_back = lax.optimization_barrier(
        (flip(send, "core"), flip(send_o, "core"), output_back)
    )
    grad_packed = join(keep, send, keep_o, send_o)
    output_back = after(output_back, grad_packed)
    grad_packed = grad_packed.reshape(2 * dps * tps * part // 2, -1)
    grad_packed = lax.psum_scatter(grad_packed, ("dp", "y"), scatter_dimension=0, tiled=True)
    grad_packed = lax.psum_scatter(grad_packed, "tp", scatter_dimension=0, tiled=True)

    layer_out = spread_rows(after(layer_rows, output_back), tps)
    dq, dkv_2, dkv_3 = attend_back(
        queries, output_back, attended, log_total, (kv_2, kv_3), biases[2:], None
    )
    far = add_low(dkv_2, flip(dkv_3, "core"))
    dq = after(dq, far)
    far = flip(far, "y")
    dq, dkv_0, dkv_1 = attend_back(
        queries, output_back, attended, log_total, (kv, kv_1), biases[:2], dq
    )
    dkv_1, layer_out = lax.optimization_barrier((dkv_1, layer_out))
    near = flip(dkv_1, "core")
    dkv = add_low(dkv_0, near, far)

    back = dot(dq, qkv_full[:, :local], NT) + lax.dot_general(
        dkv, qkv_full[:, local:], (((0,), (1,)), ((), ())), preferred_element_type=f32
    )
    back = swap_rows(back.astype(bf16).reshape(tps, rows, model))
    grad_qkv = jnp.concatenate(
        (
            lax.dot_general(normed, dq, (((0,), (0,)), ((), ())), preferred_element_type=f32),
            lax.dot_general(normed, dkv, (((0,), (1,)), ((), ())), preferred_element_type=f32),
        ),
        axis=1,
    ).astype(bf16)
    grad_qkv = reduce_projections(grad_qkv, dps).astype(f32)
    grad_w_qkv = jnp.stack([grad_qkv[:, i * local : (i + 1) * local] for i in range(3)])

    e = jnp.sum(back.astype(f32), axis=0)
    mine = lax.dynamic_slice_in_dim(flat, tp * rows, rows, 0).astype(f32) + embedded
    center = mine - jnp.mean(mine, axis=1, keepdims=True)
    scale = lax.rsqrt(jnp.mean(center * center, axis=1, keepdims=True) + norm_eps)
    n = center * scale
    eg = e * gain_first
    start_norm = scale * (
        eg - jnp.mean(eg, axis=1, keepdims=True) - n * jnp.mean(eg * n, axis=1, keepdims=True)
    )
    grad_rows = middle_back + start_norm
    grad_tokens = spread_rows(grad_rows.astype(bf16), tps).astype(f32)

    token_sums = jnp.zeros((dps, model), f32)
    token_sums = lax.dynamic_update_slice_in_dim(
        token_sums, jnp.sum(grad_rows, axis=0, keepdims=True), dp, 0
    )
    qv_sums = jnp.concatenate(
        (jnp.sum(dq.astype(f32), axis=0), jnp.sum(dkv[local:].astype(f32), axis=1))
    )
    qv_slots = jnp.zeros((tps, 2 * local), f32)
    qv_slots = lax.dynamic_update_slice_in_dim(qv_slots, qv_sums[None], tp, 0)
    sums = jnp.concatenate(
        (
            vectors[:4],
            jnp.sum(e * n, axis=0, keepdims=True),
            jnp.sum(e, axis=0, keepdims=True),
            token_sums,
            grad_b_up.reshape(-1, model),
            qv_slots.reshape(-1, model),
        )
    )
    sums = after(sums, grad_packed)
    grad_packed = pair(grad_packed, "y", 0)
    grad_other = flip(grad_packed, "core")
    grad_w_up, grad_w_down, grad_w_out = unpack(
        grad_packed, grad_other, core, wide // 2, local // 2
    )
    sums = sum_vectors(sums, dps, tps, grad_other)
    own = lax.dynamic_slice_in_dim(sums, dp * part, part, 1)
    grad_gains = jnp.stack((own[4], own[0]))
    grad_shifts = jnp.stack((own[5], own[1]))
    grad_out_biases = jnp.stack((own[2], own[3]))
    at = 6 + dps
    b_rows = grad_b_up.size // model
    grad_b_up = lax.dynamic_slice_in_dim(
        sums[at : at + b_rows].reshape(-1), tp * wide, wide, 0
    )
    grad_b_qv = lax.dynamic_index_in_dim(
        sums[at + b_rows :].reshape(tps, 2, local), tp, 0, False
    )
    step_rows = jnp.arange(steps_in_table)[:, None]
    grad_table = jnp.zeros((steps_in_table, part), f32)
    for s in range(dps):
        grad_table = grad_table + jnp.where(step_rows == all_steps[s], own[6 + s][None], 0.0)
    return (
        layer_out[None],
        grad_tokens[None],
        grad_table,
        grad_gains,
        grad_shifts,
        grad_w_qkv,
        grad_b_qv,
        grad_w_out,
        grad_out_biases,
        grad_w_up,
        grad_b_up,
        grad_w_down,
    )


def solution(mesh):
    in_specs = (
        P("dp", ("y", "core"), None),
        P("dp"),
        P("dp"),
        P(None, "dp"),
        P(None, "dp"),
        P(None, "dp"),
        P(None, "dp", "tp"),
        P(None, "tp"),
        P("tp", "dp"),
        P(None, "dp"),
        P("dp", "tp"),
        P("tp"),
        P("tp", "dp"),
        P("dp", ("y", "core"), None),
    )
    out_specs = (
        P("dp", ("y", "core"), None),
        P("dp", ("y", "core"), None),
        P(None, "dp"),
        P(None, "dp"),
        P(None, "dp"),
        P(None, "dp", "tp"),
        P(None, "tp"),
        P("tp", "dp"),
        P(None, "dp"),
        P("dp", "tp"),
        P("tp"),
        P("tp", "dp"),
    )
    sizes = (mesh.shape["dp"], mesh.shape["tp"])
    fine = jax.sharding.Mesh(
        mesh.devices.reshape(sizes[0], 2, mesh.shape["ctx"] // 2, sizes[1]),
        ("dp", "y", "core", "tp"),
    )
    return jax.shard_map(
        functools.partial(on_device, *sizes),
        mesh=fine,
        in_specs=in_specs,
        out_specs=out_specs,
        check_vma=False,
    )
```

```python
import functools

import jax
import jax.numpy as jnp
from jax import lax
from jax.experimental import pallas as pl
from jax.experimental.pallas import tpu as pltpu
from jax.sharding import PartitionSpec as P

HEAD = 64
norm_eps = 1e-05
NT = (((1,), (1,)), ((), ()))
NN = (((1,), (0,)), ((), ()))
f32 = jnp.float32
bf16 = jnp.bfloat16
KERNEL_VMEM = 60 * 2**20


def dot(a, b, dims=NN):
    return lax.dot_general(a, b, dims, preferred_element_type=f32)


def attend_body(heads, piece, blocks, first, last, q_ref, *refs):
    kv_refs, bias_refs, refs = refs[:blocks], refs[blocks : 2 * blocks], refs[2 * blocks :]
    if not first:
        (part_ref, old_ref), refs = refs[:2], refs[2:]
    out_ref, stat_ref, score_ref = refs[0], refs[1], refs[-1]
    rows = q_ref.shape[0]
    length = kv_refs[0].shape[1]
    width = heads * HEAD
    pieces = [(b, c) for b in range(blocks) for c in range(0, length, piece)]
    stats = []
    for h in range(heads):
        cols = slice(h * HEAD, (h + 1) * HEAD)
        vals = slice(width + h * HEAD, width + (h + 1) * HEAD)
        q = q_ref[:, cols]
        peak = None
        for b, c in pieces:
            scores = dot(q, kv_refs[b][cols, c : c + piece]) + bias_refs[b][:, c : c + piece]
            score_ref[h, :, b * length + c : b * length + c + piece] = scores
            for j in range(0, piece, 128):
                part = scores[:, j : j + 128]
                peak = part if peak is None else jnp.maximum(peak, part)
        peak = jnp.max(peak, axis=1, keepdims=True)
        if not first:
            old_peak = old_ref[:, h : h + 1]
            peak = jnp.maximum(peak, old_peak)
        total, summed = None, None
        for b, c in pieces:
            weights = jnp.exp(score_ref[h, :, b * length + c : b * length + c + piece] - peak)
            for j in range(0, piece, 128):
                part = weights[:, j : j + 128]
                total = part if total is None else total + part
            part = dot(weights.astype(bf16), kv_refs[b][vals, c : c + piece], NT)
            summed = part if summed is None else summed + part
        total = jnp.sum(total, axis=1, keepdims=True)
        if not first:
            shrink = jnp.exp(old_peak - peak)
            total = total + old_ref[:, 8 + h : 9 + h] * shrink
            summed = summed + part_ref[:, cols] * shrink
        if last:
            summed = summed / total
        stats.append((peak, total))
        out_ref[:, cols] = summed
        if last:
            refs[2][:, cols] = summed.astype(bf16)
    lane = lax.broadcasted_iota(jnp.int32, (rows, 128), 1)
    packed = jnp.zeros((rows, 128), f32)
    for h, (peak, total) in enumerate(stats):
        if last:
            packed = jnp.where(lane == h, peak + jnp.log(total), packed)
        else:
            packed = jnp.where(lane == h, peak, packed)
            packed = jnp.where(lane == 8 + h, total, packed)
    stat_ref[...] = packed


def row_spec(rows, width):
    return pl.BlockSpec((rows, width), lambda i: (i, 0))


def whole_spec(array):
    zeros = (0,) * array.ndim
    return pl.BlockSpec(array.shape, lambda i: zeros)


def attend(queries, kvs, biases, carry, last, rows=128, piece=512):
    count, width = queries.shape
    length = kvs[0].shape[1]
    heads = width // HEAD
    keys = length * len(kvs)
    args = [queries, *kvs, *biases]
    specs = [row_spec(rows, width)] + [whole_spec(a) for a in args[1:]]
    if carry is not None:
        args += list(carry)
        specs += [row_spec(rows, width), row_spec(rows, 128)]
    return pl.pallas_call(
        functools.partial(attend_body, heads, piece, len(kvs), carry is None, last),
        grid=(count // rows,),
        in_specs=specs,
        out_specs=[row_spec(rows, width), row_spec(rows, 128)]
        + [row_spec(rows, width)] * last,
        out_shape=[
            jax.ShapeDtypeStruct((count, width), f32),
            jax.ShapeDtypeStruct((count, 128), f32),
        ]
        + [jax.ShapeDtypeStruct((count, width), bf16)] * last,
        scratch_shapes=[pltpu.VMEM((heads, rows, keys), f32)],
        cost_estimate=pl.CostEstimate(
            flops=16 * count * keys * width,
            bytes_accessed=count * width * 6 + keys * width * 4,
            transcendentals=count * keys * heads,
        ),
        compiler_params=pltpu.CompilerParams(vmem_limit_bytes=KERNEL_VMEM),
        name="attend",
    )(*args)


def attend_back_body(heads, piece, blocks, first, q_ref, do_ref, att_ref, log_ref, *refs):
    kv_refs, bias_refs, refs = refs[:blocks], refs[blocks : 2 * blocks], refs[2 * blocks :]
    if not first:
        part_ref, refs = refs[0], refs[1:]
    dq_ref, dkv_refs, sum_refs = refs[0], refs[1 : 1 + blocks], refs[1 + blocks :]
    step = pl.program_id(0)
    length = kv_refs[0].shape[1]
    width = heads * HEAD

    @pl.when(step == 0)
    def _():
        for sum_ref in sum_refs:
            sum_ref[...] = jnp.zeros_like(sum_ref)

    q, do = q_ref[...], do_ref[...]
    q_t, do_t = q.T, do.T
    product = do.astype(f32) * att_ref[...]
    for h in range(heads):
        cols = slice(h * HEAD, (h + 1) * HEAD)
        vals = slice(width + h * HEAD, width + (h + 1) * HEAD)
        delta = jnp.sum(product[:, cols], axis=1, keepdims=True)
        log_total = log_ref[:, h : h + 1]
        dq = None
        for b in range(blocks):
            for c in range(0, length, piece):
                span = slice(c, c + piece)
                scores = dot(q[:, cols], kv_refs[b][cols, span]) + bias_refs[b][:, span]
                probs = jnp.exp(scores - log_total)
                grads = dot(do[:, cols], kv_refs[b][vals, span])
                score_grad = (probs * (grads - delta)).astype(bf16)
                part = dot(score_grad, kv_refs[b][cols, span], NT)
                dq = part if dq is None else dq + part
                sum_refs[b][cols, span] += dot(q_t[cols, :], score_grad)
                sum_refs[b][vals, span] += dot(do_t[cols, :], probs.astype(bf16))
        dq = dq * HEAD ** (-0.5)
        if not first:
            dq = dq + part_ref[:, cols]
        dq_ref[:, cols] = dq.astype(dq_ref.dtype)

    @pl.when(step == pl.num_programs(0) - 1)
    def _():
        for dkv_ref, sum_ref in zip(dkv_refs, sum_refs):
            dkv_ref[...] = sum_ref[...].astype(dkv_ref.dtype)


def attend_back(queries, do, att, log_total, kvs, biases, part, rows=256, piece=1024):
    count, width = queries.shape
    length = kvs[0].shape[1]
    heads = width // HEAD
    keys = length * len(kvs)
    args = [queries, do, att, log_total, *kvs, *biases]
    specs = [row_spec(rows, width)] * 3 + [row_spec(rows, 128)]
    specs += [whole_spec(a) for a in args[4:]]
    if part is not None:
        args.append(part)
        specs.append(row_spec(rows, width))
    return pl.pallas_call(
        functools.partial(attend_back_body, heads, piece, len(kvs), part is None),
        grid=(count // rows,),
        in_specs=specs,
        out_specs=[row_spec(rows, width)] + [whole_spec(kv) for kv in kvs],
        out_shape=[jax.ShapeDtypeStruct((count, width), f32 if part is None else bf16)]
        + [jax.ShapeDtypeStruct(kv.shape, bf16) for kv in kvs],
        scratch_shapes=[pltpu.VMEM(kv.shape, f32) for kv in kvs],
        cost_estimate=pl.CostEstimate(
            flops=4 * count * keys * width,
            bytes_accessed=count * width * 12 + keys * width * 8,
            transcendentals=count * keys * heads,
        ),
        compiler_params=pltpu.CompilerParams(vmem_limit_bytes=KERNEL_VMEM),
        name="attend_back",
    )(*args)


def middle_body(
    num_ref, att_ref, tok_ref, emb_ref, par_ref, cot_ref, wout_ref, w_ref,
    layer_ref, back_ref, do_ref, keep_ref, send_ref, keepo_ref, sendo_ref, vec_ref, bvec_ref,
    mid_ref, sec_ref, sect_ref, upl_ref, uplt_ref, mlp_ref, sback_ref,
):
    step = pl.program_id(0)
    tps, rows, width = att_ref.shape
    model = tok_ref.shape[1]
    wide = w_ref.shape[2] // 2
    blocks, sub = keep_ref.shape[0], keep_ref.shape[2]
    low_core = num_ref[3] == 0

    def store(keep, send, left, right, t, at):
        half = right.shape[1] // 2
        low, high = right[:, :half], right[:, half:]
        for ref, chosen in (
            (keep, jnp.where(low_core, low, high)),
            (send, jnp.where(low_core, high, low)),
        ):
            value = dot(left, chosen)
            for b in range(blocks):
                ref[b, t, :, at : at + half] = value[b * sub : (b + 1) * sub].astype(bf16)

    @pl.when(step == 0)
    def _():
        start = tok_ref[...].astype(f32) + emb_ref[...]
        attn = None
        for t in range(tps):
            part = dot(att_ref[t], wout_ref[t][:, :width], NT)
            attn = part if attn is None else attn + part
        middle = start + attn + par_ref[2:3, :]
        mid_ref[...] = middle
        center = middle - jnp.mean(middle, axis=1, keepdims=True)
        scale = lax.rsqrt(jnp.mean(center * center, axis=1, keepdims=True) + norm_eps)
        second = (center * scale * par_ref[0:1, :] + par_ref[1:2, :]).astype(bf16)
        sec_ref[...] = second
        sect_ref[...] = second.T
        place = num_ref[0] + lax.broadcasted_iota(jnp.int32, (rows, model), 0)
        upstream = jnp.where(place < num_ref[1], cot_ref[...].astype(f32), 0.0)
        low = upstream.astype(bf16)
        upl_ref[...] = low
        uplt_ref[...] = low.T
        mlp_ref[...] = jnp.zeros_like(mlp_ref)
        sback_ref[...] = jnp.zeros_like(sback_ref)

    w_up, w_down = w_ref[0, :, :wide], w_ref[0, :, wide:]
    b_up = wout_ref[step][:, width:].astype(f32).T[0:1, :]
    hidden = dot(sec_ref[...], w_up) + b_up
    half = 0.5 * (1.0 + lax.erf(hidden * (0.5**0.5)))
    activated = (hidden * half).astype(bf16)
    mlp_ref[...] += dot(activated, w_down, NT)
    act_back = dot(upl_ref[...], w_down)
    slope = half + hidden * (jnp.exp(-0.5 * hidden * hidden) * 0.3989422804014327)
    hidden_back = (act_back * slope).astype(bf16)
    sback_ref[...] += dot(hidden_back, w_up, NT)
    bvec_ref[pl.ds(step, 1), :] = jnp.sum(hidden_back.astype(f32), axis=0, keepdims=True)
    store(keep_ref, send_ref, sect_ref[...], hidden_back, 0, 0)
    store(keep_ref, send_ref, uplt_ref[...], activated, 0, wide // 2)

    @pl.when(step == pl.num_programs(0) - 1)
    def _():
        middle = mid_ref[...]
        layer_ref[...] = (middle + mlp_ref[...] + par_ref[3:4, :]).astype(bf16)
        center = middle - jnp.mean(middle, axis=1, keepdims=True)
        scale = lax.rsqrt(jnp.mean(center * center, axis=1, keepdims=True) + norm_eps)
        n = center * scale
        e = sback_ref[...]
        eg = e * par_ref[0:1, :]
        norm = scale * (
            eg
            - jnp.mean(eg, axis=1, keepdims=True)
            - n * jnp.mean(eg * n, axis=1, keepdims=True)
        )
        upstream = upl_ref[...].astype(f32)
        back = upstream + norm
        back_ref[...] = back
        low = back.astype(bf16)
        low_t = low.T
        keepo_ref[...] = jnp.zeros_like(keepo_ref)
        sendo_ref[...] = jnp.zeros_like(sendo_ref)
        for t in range(tps):
            do_ref[t] = dot(low, wout_ref[t][:, :width]).astype(bf16)
            store(keepo_ref, sendo_ref, low_t, att_ref[t], t, 0)
        vec_ref[0:1, :] = jnp.sum(e * n, axis=0, keepdims=True)
        vec_ref[1:2, :] = jnp.sum(e, axis=0, keepdims=True)
        vec_ref[2:3, :] = jnp.sum(low.astype(f32), axis=0, keepdims=True)
        vec_ref[3:4, :] = jnp.sum(upstream, axis=0, keepdims=True)
        vec_ref[4:8, :] = jnp.zeros((4, model), f32)


def middle_part(numbers, att, tokens, embedded, params, cotangent, weights, wide, blocks):
    tps, rows, width = att.shape
    model = tokens.shape[1]
    packed = weights.shape[2]
    fixed = lambda shape: pl.BlockSpec(shape, lambda i, n: (0,) * len(shape))
    mine = pl.BlockSpec((rows, model), lambda i, n: (n[2], 0))
    spare = packed - 2 * wide
    sub = model // blocks
    small = (blocks, tps, sub, 128)
    moving = pl.BlockSpec((blocks, 1, sub, wide), lambda i, n: (0, i, 0, 0))
    return pl.pallas_call(
        middle_body,
        grid_spec=pltpu.PrefetchScalarGridSpec(
            num_scalar_prefetch=1,
            grid=(tps,),
            in_specs=[
                fixed(att.shape),
                mine,
                fixed(embedded.shape),
                fixed(params.shape),
                mine,
                pl.BlockSpec((tps, model, spare), lambda i, n: (0, 0, 2 * wide // spare)),
                pl.BlockSpec((1, model, 2 * wide), lambda i, n: (i, 0, 0)),
            ],
            out_specs=[
                fixed((rows, model)),
                fixed((rows, model)),
                fixed(att.shape),
                moving,
                moving,
                fixed(small),
                fixed(small),
                fixed((8, model)),
                fixed((tps, wide)),
            ],
            scratch_shapes=[
                pltpu.VMEM((rows, model), f32),
                pltpu.VMEM((rows, model), bf16),
                pltpu.VMEM((model, rows), bf16),
                pltpu.VMEM((rows, model), bf16),
                pltpu.VMEM((model, rows), bf16),
                pltpu.VMEM((rows, model), f32),
                pltpu.VMEM((rows, model), f32),
            ],
        ),
        out_shape=[
            jax.ShapeDtypeStruct((rows, model), bf16),
            jax.ShapeDtypeStruct((rows, model), f32),
            jax.ShapeDtypeStruct(att.shape, bf16),
            jax.ShapeDtypeStruct((blocks, tps, sub, wide), bf16),
            jax.ShapeDtypeStruct((blocks, tps, sub, wide), bf16),
            jax.ShapeDtypeStruct(small, bf16),
            jax.ShapeDtypeStruct(small, bf16),
            jax.ShapeDtypeStruct((8, model), f32),
            jax.ShapeDtypeStruct((tps, wide), f32),
        ],
        cost_estimate=pl.CostEstimate(
            flops=12 * rows * model * wide * tps,
            bytes_accessed=2 * weights.size * 2,
            transcendentals=2 * rows * wide * tps,
        ),
        compiler_params=pltpu.CompilerParams(vmem_limit_bytes=KERNEL_VMEM),
        name="middle",
    )(numbers, att, tokens, embedded, params, cotangent, weights, weights)


def flip(value, axis, bit=1, size=2):
    return lax.ppermute(value, axis, [(i, i ^ bit) for i in range(size)])


def after(value, *others):
    return lax.optimization_barrier((value, *others))[0]


def swap_rows(value):
    return lax.all_to_all(value, "tp", 0, 0, tiled=True)


def gather_dp(value, dps, axis):
    if dps != 2:
        return lax.all_gather(value, "dp", axis=axis, tiled=True)
    return pair(value, "dp", axis)


def pair(value, axis_name, axis):
    other = flip(value, axis_name)
    first = lax.axis_index(axis_name) == 0
    return jnp.concatenate(
        (jnp.where(first, value, other), jnp.where(first, other, value)), axis=axis
    )


def add_low(*terms):
    total = terms[0].astype(f32)
    for term in terms[1:]:
        total = total + term.astype(f32)
    return total.astype(bf16)


def sum_vectors(value, dps, tps, then):
    for axis in ("core", "y"):
        value = value + flip(value, axis)
    value = after(value, then)
    if dps == 2:
        value = value + flip(value, "dp")
    else:
        value = lax.psum(value, "dp")
    for bit in (1, 2):
        value = value + flip(value, "tp", bit, tps)
    return value


def reduce_projections(grad, late, dps):
    if dps != 2:
        grad = lax.psum_scatter(grad, ("dp", "y", "core"), scatter_dimension=0, tiled=True)
        return lax.all_gather(grad, ("y", "core"), axis=0, tiled=True), late
    dp, y, core = lax.axis_index("dp"), lax.axis_index("y"), lax.axis_index("core")
    size = grad.shape[0] // 8
    grad = grad.reshape(2, 2, 2 * size, -1)
    pick = lambda v, i, axis: lax.dynamic_index_in_dim(v, i, axis, False)
    grad = add_low(pick(grad, core, 1), flip(pick(grad, 1 - core, 1), "core"))
    grad = add_low(pick(grad, dp, 0), flip(pick(grad, 1 - dp, 0), "dp"))
    grad = grad.reshape(2, size, -1)
    grad = add_low(pick(grad, y, 0), flip(pick(grad, 1 - y, 0), "y"))
    grad, late = lax.optimization_barrier((grad, late))
    return pair(pair(grad, "y", 0), "core", 0), late


def join_body(keep_ref, send_ref, keepo_ref, sendo_ref, out_ref):
    wide = keep_ref.shape[-1]
    for t in range(keep_ref.shape[1]):
        total = keep_ref[0, t].astype(f32) + send_ref[0, t].astype(f32)
        out_ref[0, t, :, :wide] = total.astype(bf16)
        total = keepo_ref[0, t].astype(f32) + sendo_ref[0, t].astype(f32)
        out_ref[0, t, :, wide:] = total.astype(bf16)


def join(keep, send, keep_o, send_o):
    blocks, tps, sub, wide = keep.shape
    spec = lambda last: pl.BlockSpec((1, tps, sub, last), lambda i: (i, 0, 0, 0))
    return pl.pallas_call(
        join_body,
        grid=(blocks,),
        in_specs=[spec(wide), spec(wide), spec(128), spec(128)],
        out_specs=spec(wide + 128),
        out_shape=jax.ShapeDtypeStruct((blocks, tps, sub, wide + 128), bf16),
        cost_estimate=pl.CostEstimate(
            flops=keep.size, bytes_accessed=7 * keep.size, transcendentals=0
        ),
        name="join",
    )(keep, send, keep_o, send_o)


def unpack_body(half, half_out, core_ref, mine_ref, other_ref, up_ref, down_ref, out_ref):
    low_core = core_ref[0] == 0
    mine, other = mine_ref[...].astype(f32), other_ref[...].astype(f32)
    halves = (jnp.where(low_core, mine, other), jnp.where(low_core, other, mine))
    for i, value in enumerate(halves):
        up_ref[:, i * half : (i + 1) * half] = value[:, :half]
        down_ref[i * half : (i + 1) * half, :] = value[:, half : 2 * half].T
        turned = value[:, 2 * half :].T
        out_ref[i * half_out : (i + 1) * half_out, :] = turned[:half_out]


def unpack(mine, other, core, half, half_out):
    part = mine.shape[0]
    shapes = ((part, 2 * half), (2 * half, part), (2 * half_out, part))
    if part % 128:
        first = core == 0
        halves = (jnp.where(first, mine, other), jnp.where(first, other, mine))
        pick = lambda a, b: jnp.concatenate([h[:, a:b] for h in halves], axis=1).astype(f32)
        return (
            pick(0, half),
            pick(half, 2 * half).T,
            pick(2 * half, 2 * half + half_out).T,
        )
    fixed = lambda shape: pl.BlockSpec(shape, lambda i, n: (0,) * len(shape))
    return pl.pallas_call(
        functools.partial(unpack_body, half, half_out),
        grid_spec=pltpu.PrefetchScalarGridSpec(
            num_scalar_prefetch=1,
            grid=(1,),
            in_specs=[fixed(mine.shape)] * 2,
            out_specs=[fixed(shape) for shape in shapes],
        ),
        out_shape=[jax.ShapeDtypeStruct(shape, f32) for shape in shapes],
        name="unpack",
    )(core[None].astype(jnp.int32), mine, other)


def spread_rows(value, tps):
    copies = swap_rows(jnp.broadcast_to(value[None], (tps, *value.shape)))
    return copies.reshape(tps * value.shape[0], value.shape[1])


def on_device(
    dps, tps,
    tokens, time_steps, lengths, time_table, norm_gains, norm_biases, w_qkv, b_qv, w_out,
    out_biases, w_up, b_up, w_down, cotangent,
):
    _, row_count, model = tokens.shape
    local = b_qv.shape[1]
    wide = b_up.shape[0]
    part = w_up.shape[0]
    steps_in_table = time_table.shape[0]
    rows = row_count // tps
    dp, tp = lax.axis_index("dp"), lax.axis_index("tp")
    core = lax.axis_index("core")
    ctx = 2 * lax.axis_index("y") + core

    all_steps = gather_dp(time_steps, dps, 0)
    small = jnp.concatenate((norm_gains, norm_biases, out_biases, time_table[all_steps]))
    small = gather_dp(small, dps, 1).astype(f32)
    embedded = lax.dynamic_slice_in_dim(small, 6 + dp, 1, 0)
    gain_first, shift_first = small[0:1], small[2:3]
    params = jnp.stack(
        (small[1], small[3], small[4], small[5], small[1], small[1], small[1], small[1])
    )

    qkv_mine = jnp.concatenate((w_qkv[0], w_qkv[1], w_qkv[2]), axis=1)
    qkv_full = gather_dp(qkv_mine, dps, 0)
    slab = part // 4
    spare = -(-(local + 1) // 128) * 128
    piece = jnp.concatenate(
        (
            lax.dynamic_slice_in_dim(w_up, ctx * slab, slab, 0),
            lax.dynamic_slice_in_dim(w_down, ctx * slab, slab, 1).T,
            lax.dynamic_slice_in_dim(w_out, ctx * slab, slab, 1).T,
            lax.dynamic_slice_in_dim(b_up, dp * part + ctx * slab, slab, 0)[:, None],
            jnp.zeros((slab, spare - local - 1), bf16),
        ),
        axis=1,
    )
    weights = lax.all_gather(piece, ("tp", "dp", "y", "core"), axis=0, tiled=True)
    weights = weights.reshape(tps, model, 2 * wide + spare)

    flat = tokens.reshape(row_count, model)
    start = flat.astype(f32) + embedded
    center = start - jnp.mean(start, axis=1, keepdims=True)
    scale = lax.rsqrt(jnp.mean(center * center, axis=1, keepdims=True) + norm_eps)
    normed = (center * scale * gain_first + shift_first).astype(bf16)
    bias = b_qv.astype(f32)
    kv_bias = jnp.concatenate((jnp.zeros((local,), f32), bias[1]))[:, None]
    kv = lax.dot_general(
        qkv_full[:, local:], normed, (((0,), (1,)), ((), ())), preferred_element_type=f32
    )
    kv = (kv + kv_bias).astype(bf16)
    queries = (dot(normed, qkv_full[:, :local]) + bias[0]).astype(bf16) * bf16(HEAD**-0.5)

    place = jnp.arange(row_count)[None, :]

    def key_bias(owner):
        return jnp.where(owner * row_count + place < lengths[0], 0.0, -1e30).astype(f32)

    biases = [key_bias(ctx ^ b) for b in range(4)]
    kv_1 = flip(kv, "core")
    kv_2 = flip(kv, "y")
    carry = attend(queries, (kv, kv_1), biases[:2], None, False)
    kv_2 = after(kv_2, *carry)
    kv_3 = flip(kv_2, "core")
    attended, log_total, attended_low = attend(queries, (kv_2, kv_3), biases[2:], carry, True)

    swapped = swap_rows(attended_low.reshape(tps, rows, local))
    numbers = jnp.stack((ctx * row_count + tp * rows, lengths[0], tp, core)).astype(jnp.int32)
    layer_rows, middle_back, output_back, keep, send, keep_o, send_o, vectors, grad_b_up = middle_part(
        numbers,
        swapped,
        flat,
        embedded,
        params,
        cotangent.reshape(row_count, model),
        weights,
        wide,
        2 * dps,
    )
    output_back = swap_rows(output_back).reshape(row_count, local)

    send, send_o, output_back = lax.optimization_barrier(
        (flip(send, "core"), flip(send_o, "core"), output_back)
    )
    grad_packed = join(keep, send, keep_o, send_o)
    output_back = after(output_back, grad_packed)
    grad_packed = grad_packed.reshape(2 * dps * tps * part // 2, -1)
    grad_packed = lax.psum_scatter(grad_packed, ("dp", "y"), scatter_dimension=0, tiled=True)
    grad_packed = lax.psum_scatter(grad_packed, "tp", scatter_dimension=0, tiled=True)

    layer_out = spread_rows(after(layer_rows, output_back), tps)
    dq, dkv_2, dkv_3 = attend_back(
        queries, output_back, attended, log_total, (kv_2, kv_3), biases[2:], None
    )
    far = add_low(dkv_2, flip(dkv_3, "core"))
    dq = after(dq, far)
    far = flip(far, "y")
    dq, dkv_0, dkv_1 = attend_back(
        queries, output_back, attended, log_total, (kv, kv_1), biases[:2], dq
    )
    dkv_1, layer_out = lax.optimization_barrier((dkv_1, layer_out))
    near = flip(dkv_1, "core")
    dkv = add_low(dkv_0, near, far)

    back = dot(dq, qkv_full[:, :local], NT) + lax.dot_general(
        dkv, qkv_full[:, local:], (((0,), (1,)), ((), ())), preferred_element_type=f32
    )
    back = back.astype(bf16).reshape(tps, rows, model)
    normed = after(normed, back)
    back = swap_rows(back)
    grad_qkv = jnp.concatenate(
        (
            lax.dot_general(normed, dq, (((0,), (0,)), ((), ())), preferred_element_type=f32),
            lax.dot_general(normed, dkv, (((0,), (1,)), ((), ())), preferred_element_type=f32),
        ),
        axis=1,
    ).astype(bf16)
    grad_qkv, back = reduce_projections(grad_qkv, back, dps)
    grad_qkv = grad_qkv.astype(f32)
    grad_w_qkv = jnp.stack([grad_qkv[:, i * local : (i + 1) * local] for i in range(3)])

    e = jnp.sum(back.astype(f32), axis=0)
    mine = lax.dynamic_slice_in_dim(flat, tp * rows, rows, 0).astype(f32) + embedded
    center = mine - jnp.mean(mine, axis=1, keepdims=True)
    scale = lax.rsqrt(jnp.mean(center * center, axis=1, keepdims=True) + norm_eps)
    n = center * scale
    eg = e * gain_first
    start_norm = scale * (
        eg - jnp.mean(eg, axis=1, keepdims=True) - n * jnp.mean(eg * n, axis=1, keepdims=True)
    )
    grad_rows = middle_back + start_norm
    grad_tokens = spread_rows(grad_rows.astype(bf16), tps).astype(f32)

    token_sums = jnp.zeros((dps, model), f32)
    token_sums = lax.dynamic_update_slice_in_dim(
        token_sums, jnp.sum(grad_rows, axis=0, keepdims=True), dp, 0
    )
    qv_sums = jnp.concatenate(
        (jnp.sum(dq.astype(f32), axis=0), jnp.sum(dkv[local:].astype(f32), axis=1))
    )
    qv_slots = jnp.zeros((tps, 2 * local), f32)
    qv_slots = lax.dynamic_update_slice_in_dim(qv_slots, qv_sums[None], tp, 0)
    sums = jnp.concatenate(
        (
            vectors[:4],
            jnp.sum(e * n, axis=0, keepdims=True),
            jnp.sum(e, axis=0, keepdims=True),
            token_sums,
            grad_b_up.reshape(-1, model),
            qv_slots.reshape(-1, model),
        )
    )
    sums = after(sums, grad_packed)
    grad_packed = pair(grad_packed, "y", 0)
    grad_other = flip(grad_packed, "core")
    grad_w_up, grad_w_down, grad_w_out = unpack(
        grad_packed, grad_other, core, wide // 2, local // 2
    )
    sums = sum_vectors(sums, dps, tps, grad_other)
    own = lax.dynamic_slice_in_dim(sums, dp * part, part, 1)
    grad_gains = jnp.stack((own[4], own[0]))
    grad_shifts = jnp.stack((own[5], own[1]))
    grad_out_biases = jnp.stack((own[2], own[3]))
    at = 6 + dps
    b_rows = grad_b_up.size // model
    grad_b_up = lax.dynamic_slice_in_dim(
        sums[at : at + b_rows].reshape(-1), tp * wide, wide, 0
    )
    grad_b_qv = lax.dynamic_index_in_dim(
        sums[at + b_rows :].reshape(tps, 2, local), tp, 0, False
    )
    step_rows = jnp.arange(steps_in_table)[:, None]
    grad_table = jnp.zeros((steps_in_table, part), f32)
    for s in range(dps):
        grad_table = grad_table + jnp.where(step_rows == all_steps[s], own[6 + s][None], 0.0)
    return (
        layer_out[None],
        grad_tokens[None],
        grad_table,
        grad_gains,
        grad_shifts,
        grad_w_qkv,
        grad_b_qv,
        grad_w_out,
        grad_out_biases,
        grad_w_up,
        grad_b_up,
        grad_w_down,
    )


def solution(mesh):
    in_specs = (
        P("dp", ("y", "core"), None),
        P("dp"),
        P("dp"),
        P(None, "dp"),
        P(None, "dp"),
        P(None, "dp"),
        P(None, "dp", "tp"),
        P(None, "tp"),
        P("tp", "dp"),
        P(None, "dp"),
        P("dp", "tp"),
        P("tp"),
        P("tp", "dp"),
        P("dp", ("y", "core"), None),
    )
    out_specs = (
        P("dp", ("y", "core"), None),
        P("dp", ("y", "core"), None),
        P(None, "dp"),
        P(None, "dp"),
        P(None, "dp"),
        P(None, "dp", "tp"),
        P(None, "tp"),
        P("tp", "dp"),
        P(None, "dp"),
        P("dp", "tp"),
        P("tp"),
        P("tp", "dp"),
    )
    sizes = (mesh.shape["dp"], mesh.shape["tp"])
    fine = jax.sharding.Mesh(
        mesh.devices.reshape(sizes[0], 2, mesh.shape["ctx"] // 2, sizes[1]),
        ("dp", "y", "core", "tp"),
    )
    return jax.shard_map(
        functools.partial(on_device, *sizes),
        mesh=fine,
        in_specs=in_specs,
        out_specs=out_specs,
        check_vma=False,
    )
```
